32 devices in a mesh: slides: 2 (over y), seq: 16 (over z, x, core), mp: 1.
Axes of the slice: x: 2, y: 2, z: 4, core: 2. Of those that a mesh axis runs over, the one named last changes fastest.
Arguments:
- tokens: bfloat16 [32768, 768], P(('slides', 'seq', 'mp')), parts along dimension 0, may hold values from -6 to 6
- attn_gain: float32 [768], replicated, may hold values from 0.25 to 1.75
- query_first: bfloat16 [768, 768], P(None, 'mp'), may hold values from -4 to 4
- key_first: bfloat16 [768, 768], P(None, 'mp'), may hold values from -4 to 4
- segment_value: bfloat16 [768, 768], P(None, 'mp'), may hold values from -0.21875 to 0.21875
- output_first: bfloat16 [768, 768], P('mp'), may hold values from -0.875 to 0.875
- mlp_gain: float32 [768], replicated, may hold values from 0.25 to 1.75
- up_weight: bfloat16 [768, 3072], P(None, 'mp'), may hold values from -0.21875 to 0.21875
- down_weight: bfloat16 [3072, 768], P('mp'), may hold values from -0.109375 to 0.109375
- second_gain: float32 [768], replicated, may hold values from 0.25 to 1.75
- query_second: bfloat16 [768, 768], P(None, 'mp'), may hold values from -4 to 4
- key_second: bfloat16 [768, 768], P(None, 'mp'), may hold values from -4 to 4
- value_second: bfloat16 [768, 768], P(None, 'mp'), may hold values from -0.21875 to 0.21875
- output_second: bfloat16 [768, 768], P('mp'), may hold values from -0.875 to 0.875
- segment_offset: int32 [16], P('mp'), may hold values from 0 to 63
- global_offset: int32 [16], P('mp'), may hold values from 0 to 63
Outputs:
- encoded: bfloat16 [32768, 768], P(('slides', 'seq', 'mp')), parts along dimension 0
The draws below stay inside these ranges and needn't reach their ends.
There are 2 independent parts, one for each index of `slides`. The reference program is written for one: setup_inputs(seed, part) draws one part's arguments, and reference() takes and returns one part's arrays. A program takes and returns all parts, laid end to end along the dimension named above; an argument that names none is the same for every part. Nothing has to cross between parts.
All inputs are finite; a program needn't handle non-finite values.
Results may differ from the reference program's by a relative error of at most 0.03.
The reference program's roundings to bfloat16 on the way count: a program that leaves them out, or rounds other values in their place, can miss the bound.
Values may be sent and summed in bfloat16 or wider, within the bound.
A program may use at most 128 MiB of HBM per device.

```python
import math
import jax
import jax.numpy as jnp
from jax import lax

D = 768
HEADS = 16
FF = 3072
HEAD_DIM = 48
KEYS = 256
TOK_DEV = 1024
SEG_DEV = 16
TOKENS = 16384
N_SEQ = 16


def weight_pair(key, layer):
    base_key = jax.random.fold_in(key, 7100 + layer)
    first_key, whole_sequence_key = jax.random.split(base_key, 2)
    common = jax.random.truncated_normal(first_key, -4.0, 4.0, (D, D), jnp.float32)
    spare = jax.random.truncated_normal(whole_sequence_key, -4.0, 4.0, (D, D), jnp.float32)
    query_part = common / math.sqrt(D)
    key_part = spare / math.sqrt(D)
    return (jnp.clip(query_part, -4.0, 4.0), jnp.clip(key_part, -4.0, 4.0))


def draw_query_first(key, part):
    return weight_pair(key, 1)[0].astype(jnp.bfloat16)


def draw_key_first(key, part):
    return weight_pair(key, 1)[1].astype(jnp.bfloat16)


def draw_query_second(key, part):
    return weight_pair(key, 2)[0].astype(jnp.bfloat16)


def draw_key_second(key, part):
    return weight_pair(key, 2)[1].astype(jnp.bfloat16)


def touch_ends(values, key, low, top_value):
    extent = values.shape
    spot = [jax.random.randint(jax.random.fold_in(key, axis), (), 0, extent[axis]) for axis in range(len(extent))]
    values = values.at[tuple(spot)].set(low)
    longest = extent.index(max(extent))
    spot[longest] = (spot[longest] + 1) % extent[longest]
    return values.at[tuple(spot)].set(top_value)


def levels(stream_key, dims, cuts, smallest, high):
    def one(dim, shards_of):
        steps = jax.random.uniform(jax.random.fold_in(jax.random.fold_in(stream_key, 6), dim), (shards_of,), jnp.float32, smallest / len(cuts), high / len(cuts))
        return jnp.repeat(jnp.exp(steps), dims[dim] // shards_of).reshape((-1,) + (1,) * (len(dims) - dim - 1))

    level = one(*cuts[0])
    for cut in cuts[1:]:
        level = level * one(*cut)
    return level


def gaussian(own_key, shape, scale, bound, shards=(), held_as=jnp.bfloat16):
    factor_of = levels(own_key, shape, shards, -0.22, 0.18) if shards else 1.0
    drawn = jax.random.normal(own_key, shape, jnp.float32) * scale * factor_of
    return jnp.minimum(jnp.maximum(drawn, -bound), bound).astype(held_as)


def setup_inputs(seed: int = 0, part: int = 0) -> dict:
    key_list = jax.random.split(jax.random.key(seed), 17)
    part_splits = jax.random.split(jax.random.fold_in(key_list[16], part), 17)
    tokens = gaussian(part_splits[0], (TOKENS, D), 1.0, 6.0, ((0, 16),))
    attn_gain = jnp.clip(1.0 + 0.15 * jax.random.normal(key_list[1], (D,), jnp.float32), 0.25, 1.75)
    query_first = draw_query_first(jax.random.fold_in(key_list[16], 71), part)
    key_first = draw_key_first(jax.random.fold_in(key_list[16], 71), part)
    segment_value = gaussian(key_list[4], (D, D), D ** -0.5, 0.21875)
    output_first = gaussian(key_list[5], (D, D), HEAD_DIM ** -0.5, 0.875)
    mlp_gain = jnp.clip(1.0 + 0.15 * jax.random.normal(key_list[6], (D,), jnp.float32), 0.25, 1.75)
    up_weight = gaussian(key_list[7], (D, FF), D ** -0.5, 0.21875)
    down_weight = gaussian(key_list[8], (FF, D), FF ** -0.5, 0.109375)
    second_gain = jnp.clip(1.0 + 0.15 * jax.random.normal(key_list[9], (D,), jnp.float32), 0.25, 1.75)
    query_second = draw_query_second(jax.random.fold_in(key_list[16], 71), part)
    key_second = draw_key_second(jax.random.fold_in(key_list[16], 71), part)
    value_second = gaussian(key_list[12], (D, D), D ** -0.5, 0.21875)
    output_second = gaussian(key_list[13], (D, D), HEAD_DIM ** -0.5, 0.875)
    segment_offset = touch_ends(jax.random.randint(key_list[14], (HEADS,), 0, SEG_DEV * TOK_DEV // KEYS), jax.random.fold_in(key_list[14], 1), 0, (SEG_DEV * TOK_DEV // KEYS) - 1).astype(jnp.int32)
    global_offset = touch_ends(jax.random.randint(key_list[15], (HEADS,), 0, N_SEQ * TOK_DEV // KEYS), jax.random.fold_in(key_list[15], 1), 0, (N_SEQ * TOK_DEV // KEYS) - 1).astype(jnp.int32)
    return {"tokens": tokens, "attn_gain": attn_gain, "query_first": query_first, "key_first": key_first, "segment_value": segment_value, "output_first": output_first, "mlp_gain": mlp_gain, "up_weight": up_weight, "down_weight": down_weight, "second_gain": second_gain, "query_second": query_second, "key_second": key_second, "value_second": value_second, "output_second": output_second, "segment_offset": segment_offset, "global_offset": global_offset}


def norm_rows(values, gain):
    center = values - lax.optimization_barrier(jnp.mean(values, axis=-1, keepdims=True))
    spread = lax.optimization_barrier(jnp.mean(center * center, axis=-1, keepdims=True))
    return (center * lax.rsqrt(spread + 1e-05) * gain).astype(jnp.bfloat16)

def attend(query, keys, values):
    scores = jnp.einsum('thd,khd->htk', query.astype(jnp.float32), keys.astype(jnp.float32)) * HEAD_DIM ** (-0.5)
    highest = lax.optimization_barrier(jnp.max(scores, axis=-1, keepdims=True))
    weights = jnp.exp(scores - highest)
    weights = (weights / lax.optimization_barrier(jnp.sum(weights, axis=-1, keepdims=True))).astype(jnp.bfloat16)
    return jnp.einsum('htk,khd->thd', weights.astype(jnp.float32), values.astype(jnp.float32)).astype(jnp.bfloat16)

def project(chosen, weight):
    shaped = weight.astype(jnp.float32).reshape(D, HEADS, HEAD_DIM)
    return jnp.einsum('...hd,dhe->...he', chosen.astype(jnp.float32), shaped).astype(jnp.bfloat16)

def reference(tokens, attn_gain, query_first, key_first, segment_value, output_first, mlp_gain, up_weight, down_weight, second_gain, query_second, key_second, value_second, output_second, segment_offset, global_offset):
    seg_len = SEG_DEV * TOK_DEV
    segment_count = TOKENS // seg_len
    seg_rate = seg_len // KEYS
    hidden = norm_rows(tokens.astype(jnp.float32), attn_gain)
    query = jnp.dot(hidden, query_first, preferred_element_type=jnp.float32).astype(jnp.bfloat16)
    query = query.reshape(segment_count, seg_len, HEADS, HEAD_DIM)
    positions = (jnp.arange(segment_count, dtype=jnp.int32)[:, None, None] * seg_len + jnp.arange(KEYS, dtype=jnp.int32)[None, :, None] * seg_rate + segment_offset.astype(jnp.int32)[None, None, :]).astype(jnp.int32)
    chosen = hidden[positions]
    keys = project(chosen, key_first)
    values = project(chosen, segment_value)
    mixed = lax.map(lambda items: attend(items[0], items[1], items[2]), (query, keys, values)).reshape(TOKENS, D)
    first = (tokens.astype(jnp.float32) + jnp.dot(mixed, output_first, preferred_element_type=jnp.float32)).astype(jnp.bfloat16)
    normed = norm_rows(first.astype(jnp.float32), mlp_gain)
    inner = jax.nn.gelu(jnp.dot(normed, up_weight, preferred_element_type=jnp.float32), approximate=True).astype(jnp.bfloat16)
    second_branch = (first.astype(jnp.float32) + jnp.dot(inner, down_weight, preferred_element_type=jnp.float32)).astype(jnp.bfloat16)
    hidden_two = norm_rows(second_branch.astype(jnp.float32), second_gain)
    query_two = jnp.dot(hidden_two, query_second, preferred_element_type=jnp.float32).astype(jnp.bfloat16)
    query_two = query_two.reshape(segment_count, seg_len, HEADS, HEAD_DIM)
    glob_rate = TOKENS // KEYS
    positions_two = (jnp.arange(KEYS, dtype=jnp.int32)[:, None] * glob_rate + global_offset.astype(jnp.int32)[None, :]).astype(jnp.int32)
    chosen_two = hidden_two[positions_two]
    keys_two = project(chosen_two, key_second)
    values_two = project(chosen_two, value_second)
    mixed_two = lax.map(lambda block: attend(block, keys_two, values_two), query_two).reshape(TOKENS, D)
    return (second_branch.astype(jnp.float32) + jnp.dot(mixed_two, output_second, preferred_element_type=jnp.float32)).astype(jnp.bfloat16)
```

```python
import functools
import math

import jax
import jax.numpy as jnp
from jax import lax
from jax.experimental import pallas as pl
from jax.experimental.pallas import tpu as pltpu
from jax.sharding import PartitionSpec as P

KEYS = 256
SEG_MAX = 16


def swapped(x, axis, apart):
    return lax.ppermute(x, axis, [(i, i ^ 1 << apart) for i in range(lax.axis_size(axis))])


def norm_rows(values, gain):
    center = values - jnp.mean(values, axis=-1, keepdims=True)
    spread = jnp.mean(center * center, axis=-1, keepdims=True)
    return (center * lax.rsqrt(spread + 1e-05) * gain).astype(jnp.bfloat16)


def pick_keys(hidden, offsets, stride, key_weight, value_weight):
    token_count, width = hidden.shape
    head_count = offsets.shape[0]
    head_size = key_weight.shape[1] // head_count
    grouped_rows = hidden.reshape(token_count // stride, stride, width)
    dilation_selector = (
        lax.broadcasted_iota(jnp.int32, (stride, head_count), 0) == offsets[None, :]
    ).astype(jnp.bfloat16)
    chosen = jnp.einsum(
        "nof,oj->njf", grouped_rows, dilation_selector, preferred_element_type=jnp.float32
    ).astype(jnp.bfloat16)
    key_heads = jnp.einsum(
        "xkr,rkf->xkf",
        chosen,
        key_weight.reshape(width, head_count, head_size),
        preferred_element_type=jnp.float32,
    ).astype(jnp.bfloat16)
    value_heads = jnp.einsum(
        "xkr,rkf->xkf",
        chosen,
        value_weight.reshape(width, head_count, head_size),
        preferred_element_type=jnp.float32,
    ).astype(jnp.bfloat16)
    picked = token_count // stride
    return jnp.stack(
        [
            key_heads.reshape(picked, head_count * head_size),
            value_heads.reshape(picked, head_count * head_size),
        ]
    )


def attend_local(query, keyval, head_count):
    token_count, width = query.shape
    head_size = width // head_count
    query_heads = query.reshape(token_count, head_count, head_size)
    key_heads = keyval[0].reshape(-1, head_count, head_size)
    value_heads = keyval[1].reshape(-1, head_count, head_size)
    scores = jnp.einsum(
        "thd,khd->htk", query_heads, key_heads, preferred_element_type=jnp.float32
    ) * head_size ** (-0.5)
    highest = jnp.max(scores, axis=-1, keepdims=True)
    weights = jnp.exp(scores - highest)
    weights = (weights / jnp.sum(weights, axis=-1, keepdims=True)).astype(jnp.bfloat16)
    mixed = jnp.einsum(
        "htk,khd->thd", weights, value_heads, preferred_element_type=jnp.float32
    ).astype(jnp.bfloat16)
    return mixed.reshape(token_count, width)


def merge_branch_pair(mine, other, level, token_position):
    lower = token_position >> level & 1 == 0
    return jnp.where(
        lower, jnp.concatenate((mine, other), axis=1), jnp.concatenate((other, mine), axis=1)
    )


def spread_segment(keyval, seg_span, token_position):
    for level in range(seg_span.bit_length() - 1):
        partner = swapped(keyval, "seq", level)
        keyval = merge_branch_pair(keyval, partner, level, token_position)
    return keyval


def spread_global(keyval_two):
    keyval_two = lax.all_gather(keyval_two, "seq", axis=1, tiled=True)
    return keyval_two


def combine(partial_value, residual_full, need_full):
    row_count = residual_full.shape[0] // lax.axis_size("mp")
    row_start = lax.axis_index("mp") * row_count
    share = lax.psum_scatter(partial_value, "mp", scatter_dimension=0, tiled=True)
    own_rows = lax.dynamic_slice_in_dim(residual_full, row_start, row_count, 0)
    own_rows = (own_rows.astype(jnp.float32) + share).astype(jnp.bfloat16)
    full_rows = lax.all_gather(own_rows, "mp", axis=0, tiled=True) if need_full else own_rows
    return (own_rows, full_rows)


def body(
    tokens,
    attn_gain,
    query_first,
    key_first,
    segment_value,
    output_first,
    mlp_gain,
    up_weight,
    down_weight,
    second_gain,
    query_second,
    key_second,
    value_second,
    output_second,
    segment_offset,
    global_offset,
):
    seq_count = lax.axis_size("seq")
    token_position = lax.axis_index("seq")
    seg_span = min(SEG_MAX, seq_count)
    head_count = segment_offset.shape[0]
    full_rows = lax.all_gather(tokens, "mp", axis=0, tiled=True)
    token_count = full_rows.shape[0]
    hidden = norm_rows(full_rows.astype(jnp.float32), attn_gain)
    query = jnp.dot(hidden, query_first, preferred_element_type=jnp.float32).astype(jnp.bfloat16)
    seg_stride = token_count // (KEYS // seg_span)
    keyval = pick_keys(hidden, segment_offset, seg_stride, key_first, segment_value)
    keyval = spread_segment(keyval, seg_span, token_position)
    mixed = attend_local(query, keyval, head_count)
    partial_value = jnp.dot(mixed, output_first, preferred_element_type=jnp.float32)
    own_rows, first_rows = combine(partial_value, full_rows, True)
    normed = norm_rows(first_rows.astype(jnp.float32), mlp_gain)
    inner = jax.nn.gelu(
        jnp.dot(normed, up_weight, preferred_element_type=jnp.float32), approximate=True
    ).astype(jnp.bfloat16)
    partial_value = jnp.dot(inner, down_weight, preferred_element_type=jnp.float32)
    own_rows, second_rows = combine(partial_value, first_rows, True)
    hidden_two = norm_rows(second_rows.astype(jnp.float32), second_gain)
    query_two = jnp.dot(hidden_two, query_second, preferred_element_type=jnp.float32).astype(
        jnp.bfloat16
    )
    glob_stride = token_count // (KEYS // seq_count)
    keyval_two = pick_keys(hidden_two, global_offset, glob_stride, key_second, value_second)
    keyval_two = spread_global(keyval_two)
    mixed_two = attend_local(query_two, keyval_two, head_count)
    partial_value = jnp.dot(mixed_two, output_second, preferred_element_type=jnp.float32)
    own_rows, unused_rows = combine(partial_value, second_rows, False)
    return own_rows


MESH = pl.DeviceIdType.MESH
F32 = jnp.float32
BF16 = jnp.bfloat16
WINDOW = 256
LANES = 128
GROUP = 2


def iota(shape, axis):
    return lax.broadcasted_iota(jnp.int32, shape, axis)


def dot32(a, b):
    return jnp.dot(a, b, preferred_element_type=F32)


def dot_last(a, b):
    return lax.dot_general(a, b, (((1,), (1,)), ((), ())), preferred_element_type=F32)


def dot_first(a, b):
    return lax.dot_general(a, b, (((0,), (0,)), ((), ())), preferred_element_type=F32)


def gelu(x):
    slope = math.sqrt(2.0 / math.pi)
    bend = jnp.tanh(x * (x * x * (0.044715 * slope) + slope))
    half = 0.5 * x
    return half * bend + half


class Gather:
    def __init__(self, n, buf, ssem, rsem):
        me = lax.axis_index("seq")
        self.me, self.n, self.high = me, n, n // 4
        self.buf, self.ssem, self.rsem = buf, ssem, rsem
        self.b0, self.b1, self.hi = me % 2, (me // 2) % 2, me // 4
        self.peer1 = self.hi * 4 + (1 - self.b1) * 2 + self.b0
        self.peer0 = self.hi * 4 + self.b1 * 2 + (1 - self.b0)

    def slot(self, d, b1, b0):
        return ((self.hi + self.high - d) % self.high) * 4 + b1 * 2 + b0

    def copy(self, slot, peer, k):
        return pltpu.make_async_remote_copy(
            src_ref=self.buf.at[slot],
            dst_ref=self.buf.at[slot],
            send_sem=self.ssem.at[k],
            recv_sem=self.rsem.at[slot],
            device_id={"seq": peer},
            device_id_type=MESH,
        )

    def peers(self):
        out = [((self.hi + d) % self.high) * 4 + self.b1 * 2 + self.b0 for d in range(1, self.high)]
        return out + [self.peer1, self.peer0]

    def start(self):
        h = self.high
        for d in range(1, h):
            peer = ((self.hi + d) % h) * 4 + self.b1 * 2 + self.b0
            self.copy(self.me, peer, d - 1).start()
        self.copy(self.me, self.peer1, h - 1).start()
        self.copy(self.me, self.peer0, 2 * h - 1).start()

    def second(self, d):
        h = self.high
        slot = self.slot(d, self.b1, self.b0)
        self.copy(slot, self.peer1, h - 1 + d).wait_recv()
        self.copy(slot, self.peer1, h - 1 + d).start()
        self.copy(slot, self.peer0, 2 * h - 1 + d).start()

    def third(self, d):
        slot = self.slot(d, 1 - self.b1, self.b0)
        self.copy(slot, self.peer0, 3 * self.high - 1 + d).wait_recv()
        self.copy(slot, self.peer0, 3 * self.high - 1 + d).start()

    def finish(self):
        h = self.high
        for b1 in (self.b1, 1 - self.b1):
            for d in range(h):
                slot = self.slot(d, b1, 1 - self.b0)
                self.copy(slot, self.peer0, 0).wait_recv()
        for k in range(4 * h - 1):
            self.copy(self.me, self.peer0, k).wait_send()


def head_column(offset_ref, heads, picked):
    rows = iota((heads * picked, 1), 0) // picked
    column = jnp.zeros((heads * picked, 1), jnp.int32)
    for h in range(heads):
        column = jnp.where(rows == h, offset_ref[h], column)
    return column


def kernel(
    n, heads, picked, stride,
    seg_hbm, glob_hbm, x_hbm, gain1_hbm, gain_mlp_hbm, gain2_hbm,
    wq1_hbm, wk1_hbm, wv1_hbm, wo1_hbm, up_hbm, down_hbm, wq2_hbm, wk2_hbm, wv2_hbm, wo2_hbm,
    out_ref,
    seg_ref, glob_ref, x_ref, gain1_ref, gain_mlp_ref, gain2_ref,
    wq1, wk1, wv1, wo1, up, down, wq2, wk2, wv2, wo2,
    xp, q, kva, kvb, kv2, km, vt, perm, perm_back, mix, sem,
    ssema, rsema, ssemb, rsemb, ssem2, rsem2,
):
    tokens, width = x_ref.shape
    size = width // heads
    half = LANES // 2
    chunk = heads * picked
    chunks = tokens // chunk
    keys = n * picked
    group = WINDOW // stride
    scale = size ** -0.5 * math.log2(math.e)
    side = width // 2

    pairs = [(wk1_hbm, wk1), (wv1_hbm, wv1), (wq1_hbm, wq1), (wo1_hbm, wo1), (up_hbm, up),
             (down_hbm, down), (wk2_hbm, wk2), (wv2_hbm, wv2), (wq2_hbm, wq2), (wo2_hbm, wo2),
             (seg_hbm, seg_ref), (x_hbm, x_ref), (gain1_hbm, gain1_ref), (glob_hbm, glob_ref),
             (gain_mlp_hbm, gain_mlp_ref), (gain2_hbm, gain2_ref)]
    loads = [pltpu.make_async_copy(a, b, sem.at[i]) for i, (a, b) in enumerate(pairs)]
    early = (10, 11, 12, 13, 14, 15, 0, 1)
    for i in early:
        loads[i].start()

    gather_a = Gather(n, kva, ssema, rsema)
    gather_b = Gather(n, kvb, ssemb, rsemb)
    second_gather = Gather(n, kv2, ssem2, rsem2)
    barrier = pltpu.get_barrier_semaphore()
    peers = gather_a.peers()
    for peer in peers:
        pl.semaphore_signal(barrier, inc=1, device_id={"seq": peer}, device_id_type=MESH)

    def own_heads(hidden, weight):
        full = dot32(hidden, weight[...])
        column = iota((picked, width), 1)
        total = jnp.zeros((picked, width), F32)
        for h in range(heads):
            mine = (column >= h * size) & (column < h * size + size)
            total = jnp.where(mine, full[h * picked:(h + 1) * picked], total)
        return total.astype(BF16)

    rows = iota((chunk, 1), 0)
    pick = rows % picked
    loads[10].wait()
    target = pick * stride + head_column(seg_ref, heads, picked)
    onehot = (iota((chunk, tokens), 1) == target).astype(F32).astype(BF16)
    loads[11].wait()
    loads[12].wait()
    for i in range(2, 10):
        loads[i].start()
    hidden = norm_rows(dot32(onehot, x_ref[...]), gain1_ref[...][None, :])
    me = gather_a.me
    loads[0].wait()
    key = own_heads(hidden, wk1)
    kva[me, 0:picked, :] = key[:, :side]
    kvb[me, 0:picked, :] = key[:, side:]
    loads[1].wait()
    value = own_heads(hidden, wv1)
    kva[me, picked:2 * picked, :] = value[:, :side]
    kvb[me, picked:2 * picked, :] = value[:, side:]
    pl.semaphore_wait(barrier, len(peers))
    gather_a.start()
    gather_b.start()

    for i in (13, 14, 15):
        loads[i].wait()
    glob_col = head_column(glob_ref, heads, picked)
    lane = iota((16, WINDOW), 1)
    inside = lane % stride
    chosen = jnp.zeros((16, WINDOW), F32)
    for h in range(heads):
        chosen = jnp.where(inside == glob_ref[h], 1.0, chosen)
    a, b = iota((WINDOW, WINDOW), 0), iota((WINDOW, WINDOW), 1)
    same = a // stride == b // stride
    before = jnp.where(same & (a < b), 1.0, 0.0).astype(BF16)
    count = dot32(chosen.astype(BF16), before)
    total = dot32(chosen.astype(BF16), jnp.where(same, 1.0, 0.0).astype(BF16))
    rank = jnp.where(chosen > 0.5, count, total + inside.astype(F32) - count)
    rank_row = rank[0:1, :]
    table = jnp.where(same & (rank_row == (a % stride).astype(F32)), 1.0, 0.0)
    perm[...] = table.astype(BF16)
    perm_back[...] = table.T.astype(BF16)
    at_head = (iota((chunk, WINDOW), 1) == glob_col)
    head_rank = jnp.sum(jnp.where(at_head, rank_row, 0.0), axis=1, keepdims=True)
    spot = (pick * heads).astype(F32) + head_rank
    onehot_two = (iota((chunk, chunk), 1).astype(F32) == spot).astype(F32).astype(BF16)

    for g in range(tokens // WINDOW):
        moved = dot32(perm[...], x_ref[g * WINDOW:(g + 1) * WINDOW, :]).astype(BF16)
        for j in range(group):
            for c in range(chunks):
                at = c * chunk + (g * group + j) * heads
                xp[at:at + heads, :] = moved[j * stride + c * heads:j * stride + (c + 1) * heads]

    def window_of(h):
        return min(h * size // LANES * LANES, width - WINDOW)

    for h in range(heads):
        km[h] = jnp.zeros((WINDOW, keys), BF16)
        vt[h * half + size:(h + 1) * half, :] = jnp.ones((half - size, keys), BF16)

    loads[2].wait()
    loads[3].wait()
    high = gather_a.high

    def query_chunk(c, carry):
        at = pl.ds(pl.multiple_of(c * chunk, chunk), chunk)
        hidden = norm_rows(xp[at, :].astype(F32), gain1_ref[...][None, :])
        q[at, :] = dot32(hidden, wq1[...]).astype(BF16)
        for d in range(1, high):
            @pl.when(c == d % chunks)
            def _(d=d):
                gather_a.second(d)

        return carry

    lax.fori_loop(0, chunks, query_chunk, 0)
    gather_a.third(0)
    gather_b.second(1)
    for d in range(1, high):
        gather_a.third(d)
    for d in range(2, high):
        gather_b.second(d)
    gather_a.finish()

    def set_keys(kv, first, last):
        span = (last - first) * size
        key = kv[:, 0:picked, :].reshape(keys, span).astype(F32).T.astype(BF16)
        value = kv[:, picked:2 * picked, :].reshape(keys, span).astype(F32).T.astype(BF16)
        for h in range(first, last):
            begin = h * size - window_of(h)
            at = (h - first) * size
            km[h, begin:begin + size, :] = key[at:at + size, :]
            vt[h * half:h * half + size, :] = value[at:at + size, :]

    def attend(c, first, last):
        at = pl.ds(pl.multiple_of(c * chunk, chunk), chunk)

        def score(h):
            start = window_of(h)
            return dot32(q[at, start:start + WINDOW], km[h])

        def soften(scores):
            top = jnp.max(scores, axis=-1, keepdims=True)
            return jnp.exp2((scores - top) * scale).astype(BF16)

        def blend(h, weights):
            both = dot_last(vt[h * half:(h + 1) * half, :], weights)
            mixed = both[:size] * (1.0 / both[size:size + 1])
            mix[c, h * size:(h + 1) * size, :] = mixed.astype(BF16)

        steps = (last - first) // GROUP
        scores, weights = {}, {}
        for i in range(steps + 2):
            if i < steps:
                for h in range(first + i * GROUP, first + (i + 1) * GROUP):
                    scores[h] = score(h)
            if 1 <= i <= steps:
                for h in range(first + (i - 1) * GROUP, first + i * GROUP):
                    weights[h] = soften(scores.pop(h))
            if i >= 2:
                for h in range(first + (i - 2) * GROUP, first + (i - 1) * GROUP):
                    blend(h, weights.pop(h))

    set_keys(kva, 0, heads // 2)

    def early_chunk(c, carry):
        attend(c, 0, heads // 2)
        for d in range(high):
            @pl.when(c == d % chunks)
            def _(d=d):
                gather_b.third(d)

        return carry

    lax.fori_loop(0, chunks, early_chunk, 0)
    gather_b.finish()
    set_keys(kvb, heads // 2, heads)
    loads[4].wait()
    loads[5].wait()
    loads[6].wait()
    loads[7].wait()
    loads[8].wait()

    def first_chunk(c, carry):
        at = pl.ds(pl.multiple_of(c * chunk, chunk), chunk)
        attend(c, heads // 2, heads)
        first = (xp[at, :].astype(F32) + dot_first(mix[c], wo1[...])).astype(BF16)
        total = first.astype(F32)
        normed = norm_rows(total, gain_mlp_ref[...][None, :])
        blocks = up.shape[1] // WINDOW
        units = {}
        for j in range(blocks + 1):
            if j < blocks:
                part = dot32(normed, up[:, j * WINDOW:(j + 1) * WINDOW])
                units[j] = gelu(part).astype(BF16)
            if j >= 1:
                total = total + dot32(units.pop(j - 1), down[(j - 1) * WINDOW:j * WINDOW, :])
        second = total.astype(BF16)
        xp[at, :] = second
        hidden_two = norm_rows(second.astype(F32), gain2_ref[...][None, :])
        q[at, :] = dot32(hidden_two, wq2[...]).astype(BF16)

        @pl.when(c == 0)
        def _():
            picked_rows = dot32(onehot_two, hidden_two).astype(BF16)
            kv2[me, 0:picked, :] = own_heads(picked_rows, wk2)
            kv2[me, picked:2 * picked, :] = own_heads(picked_rows, wv2)
            second_gather.start()

        @pl.when(c == 1)
        def _():
            for d in range(1, high):
                second_gather.second(d)

        @pl.when(c == 2)
        def _():
            for d in range(high):
                second_gather.third(d)

        return carry

    lax.fori_loop(0, chunks, first_chunk, 0)
    loads[9].wait()
    second_gather.finish()
    set_keys(kv2, 0, heads)

    def last_chunk(c, carry):
        at = pl.ds(pl.multiple_of(c * chunk, chunk), chunk)
        attend(c, 0, heads)
        xp[at, :] = (xp[at, :].astype(F32) + dot_first(mix[c], wo2[...])).astype(BF16)
        return carry

    lax.fori_loop(0, chunks, last_chunk, 0)
    for g in range(tokens // WINDOW):
        blocks = []
        for j in range(group):
            for c in range(chunks):
                at = c * chunk + (g * group + j) * heads
                blocks.append(xp[at:at + heads, :])
        moved = dot32(perm_back[...], jnp.concatenate(blocks, axis=0))
        out_ref[g * WINDOW:(g + 1) * WINDOW, :] = moved.astype(BF16)


def whole_body(
    tokens, attn_gain, query_first, key_first, segment_value, output_first, mlp_gain, up_weight,
    down_weight, second_gain, query_second, key_second, value_second, output_second,
    segment_offset, global_offset,
):
    n = lax.axis_size("seq")
    heads = segment_offset.shape[0]
    picked = KEYS // n
    count, width = tokens.shape
    stride = count // picked
    units = up_weight.shape[1]
    chunk = heads * picked
    outside = pl.BlockSpec(memory_space=pltpu.HBM)
    vmem = pl.BlockSpec(memory_space=pltpu.VMEM)
    square = pltpu.VMEM((width, width), BF16)
    gain = pltpu.VMEM((width,), F32)
    part = pltpu.VMEM((n, 2 * picked, width // 2), BF16)
    links = pltpu.SemaphoreType.DMA((n,))
    return pl.pallas_call(
        functools.partial(kernel, n, heads, picked, stride),
        out_shape=jax.ShapeDtypeStruct(tokens.shape, tokens.dtype),
        in_specs=[outside] * 16,
        out_specs=vmem,
        scratch_shapes=[
            pltpu.SMEM((heads,), jnp.int32), pltpu.SMEM((heads,), jnp.int32),
            pltpu.VMEM((count, width), BF16),
            gain, gain, gain,
            square, square, square, square,
            pltpu.VMEM((width, units), BF16), pltpu.VMEM((units, width), BF16),
            square, square, square, square,
            pltpu.VMEM((count, width), BF16),
            pltpu.VMEM((count, width), BF16),
            part, part,
            pltpu.VMEM((n, 2 * picked, width), BF16),
            pltpu.VMEM((heads, WINDOW, KEYS), BF16),
            pltpu.VMEM((heads * LANES // 2, KEYS), BF16),
            pltpu.VMEM((WINDOW, WINDOW), BF16),
            pltpu.VMEM((WINDOW, WINDOW), BF16),
            pltpu.VMEM((count // chunk, width, chunk), BF16),
            pltpu.SemaphoreType.DMA((16,)),
            links, links, links, links, links, links,
        ],
        compiler_params=pltpu.CompilerParams(
            collective_id=0, has_side_effects=True, vmem_limit_bytes=60 << 20
        ),
        name="encoder",
    )(
        segment_offset, global_offset, tokens, attn_gain, mlp_gain, second_gain,
        query_first, key_first, segment_value, output_first, up_weight, down_weight,
        query_second, key_second, value_second, output_second,
    )


def fits(mesh):
    n = mesh.shape["seq"]
    return mesh.shape["mp"] == 1 and n == SEG_MAX


def choose(mesh):
    return whole_body if fits(mesh) else body


def solution(mesh):
    placed = (
        P(("slides", "seq", "mp"), None),
        P(),
        P(None, "mp"),
        P(None, "mp"),
        P(None, "mp"),
        P("mp", None),
        P(),
        P(None, "mp"),
        P("mp", None),
        P(),
        P(None, "mp"),
        P(None, "mp"),
        P(None, "mp"),
        P("mp", None),
        P("mp"),
        P("mp"),
    )
    return jax.shard_map(
        choose(mesh),
        mesh=mesh,
        in_specs=placed,
        out_specs=P(("slides", "seq", "mp"), None),
        check_vma=False,
    )
```

```python
import functools
import math

import jax
import jax.numpy as jnp
from jax import lax
from jax.experimental import pallas as pl
from jax.experimental.pallas import tpu as pltpu
from jax.sharding import PartitionSpec as P

KEYS = 256
SEG_MAX = 16


def swapped(x, axis, apart):
    return lax.ppermute(x, axis, [(i, i ^ 1 << apart) for i in range(lax.axis_size(axis))])


def norm_rows(values, gain):
    center = values - jnp.mean(values, axis=-1, keepdims=True)
    spread = jnp.mean(center * center, axis=-1, keepdims=True)
    return (center * lax.rsqrt(spread + 1e-05) * gain).astype(jnp.bfloat16)


def pick_keys(hidden, offsets, stride, key_weight, value_weight):
    token_count, width = hidden.shape
    head_count = offsets.shape[0]
    head_size = key_weight.shape[1] // head_count
    grouped_rows = hidden.reshape(token_count // stride, stride, width)
    dilation_selector = (
        lax.broadcasted_iota(jnp.int32, (stride, head_count), 0) == offsets[None, :]
    ).astype(jnp.bfloat16)
    chosen = jnp.einsum(
        "nof,oj->njf", grouped_rows, dilation_selector, preferred_element_type=jnp.float32
    ).astype(jnp.bfloat16)
    key_heads = jnp.einsum(
        "xkr,rkf->xkf",
        chosen,
        key_weight.reshape(width, head_count, head_size),
        preferred_element_type=jnp.float32,
    ).astype(jnp.bfloat16)
    value_heads = jnp.einsum(
        "xkr,rkf->xkf",
        chosen,
        value_weight.reshape(width, head_count, head_size),
        preferred_element_type=jnp.float32,
    ).astype(jnp.bfloat16)
    picked = token_count // stride
    return jnp.stack(
        [
            key_heads.reshape(picked, head_count * head_size),
            value_heads.reshape(picked, head_count * head_size),
        ]
    )


def attend_local(query, keyval, head_count):
    token_count, width = query.shape
    head_size = width // head_count
    query_heads = query.reshape(token_count, head_count, head_size)
    key_heads = keyval[0].reshape(-1, head_count, head_size)
    value_heads = keyval[1].reshape(-1, head_count, head_size)
    scores = jnp.einsum(
        "thd,khd->htk", query_heads, key_heads, preferred_element_type=jnp.float32
    ) * head_size ** (-0.5)
    highest = jnp.max(scores, axis=-1, keepdims=True)
    weights = jnp.exp(scores - highest)
    weights = (weights / jnp.sum(weights, axis=-1, keepdims=True)).astype(jnp.bfloat16)
    mixed = jnp.einsum(
        "htk,khd->thd", weights, value_heads, preferred_element_type=jnp.float32
    ).astype(jnp.bfloat16)
    return mixed.reshape(token_count, width)


def merge_branch_pair(mine, other, level, token_position):
    lower = token_position >> level & 1 == 0
    return jnp.where(
        lower, jnp.concatenate((mine, other), axis=1), jnp.concatenate((other, mine), axis=1)
    )


def spread_segment(keyval, seg_span, token_position):
    for level in range(seg_span.bit_length() - 1):
        partner = swapped(keyval, "seq", level)
        keyval = merge_branch_pair(keyval, partner, level, token_position)
    return keyval


def spread_global(keyval_two):
    keyval_two = lax.all_gather(keyval_two, "seq", axis=1, tiled=True)
    return keyval_two


def combine(partial_value, residual_full, need_full):
    row_count = residual_full.shape[0] // lax.axis_size("mp")
    row_start = lax.axis_index("mp") * row_count
    share = lax.psum_scatter(partial_value, "mp", scatter_dimension=0, tiled=True)
    own_rows = lax.dynamic_slice_in_dim(residual_full, row_start, row_count, 0)
    own_rows = (own_rows.astype(jnp.float32) + share).astype(jnp.bfloat16)
    full_rows = lax.all_gather(own_rows, "mp", axis=0, tiled=True) if need_full else own_rows
    return (own_rows, full_rows)


def body(
    tokens,
    attn_gain,
    query_first,
    key_first,
    segment_value,
    output_first,
    mlp_gain,
    up_weight,
    down_weight,
    second_gain,
    query_second,
    key_second,
    value_second,
    output_second,
    segment_offset,
    global_offset,
):
    seq_count = lax.axis_size("seq")
    token_position = lax.axis_index("seq")
    seg_span = min(SEG_MAX, seq_count)
    head_count = segment_offset.shape[0]
    full_rows = lax.all_gather(tokens, "mp", axis=0, tiled=True)
    token_count = full_rows.shape[0]
    hidden = norm_rows(full_rows.astype(jnp.float32), attn_gain)
    query = jnp.dot(hidden, query_first, preferred_element_type=jnp.float32).astype(jnp.bfloat16)
    seg_stride = token_count // (KEYS // seg_span)
    keyval = pick_keys(hidden, segment_offset, seg_stride, key_first, segment_value)
    keyval = spread_segment(keyval, seg_span, token_position)
    mixed = attend_local(query, keyval, head_count)
    partial_value = jnp.dot(mixed, output_first, preferred_element_type=jnp.float32)
    own_rows, first_rows = combine(partial_value, full_rows, True)
    normed = norm_rows(first_rows.astype(jnp.float32), mlp_gain)
    inner = jax.nn.gelu(
        jnp.dot(normed, up_weight, preferred_element_type=jnp.float32), approximate=True
    ).astype(jnp.bfloat16)
    partial_value = jnp.dot(inner, down_weight, preferred_element_type=jnp.float32)
    own_rows, second_rows = combine(partial_value, first_rows, True)
    hidden_two = norm_rows(second_rows.astype(jnp.float32), second_gain)
    query_two = jnp.dot(hidden_two, query_second, preferred_element_type=jnp.float32).astype(
        jnp.bfloat16
    )
    glob_stride = token_count // (KEYS // seq_count)
    keyval_two = pick_keys(hidden_two, global_offset, glob_stride, key_second, value_second)
    keyval_two = spread_global(keyval_two)
    mixed_two = attend_local(query_two, keyval_two, head_count)
    partial_value = jnp.dot(mixed_two, output_second, preferred_element_type=jnp.float32)
    own_rows, unused_rows = combine(partial_value, second_rows, False)
    return own_rows


MESH = pl.DeviceIdType.MESH
F32 = jnp.float32
BF16 = jnp.bfloat16
WINDOW = 256
LANES = 128
GROUP = 2


def iota(shape, axis):
    return lax.broadcasted_iota(jnp.int32, shape, axis)


def dot32(a, b):
    return jnp.dot(a, b, preferred_element_type=F32)


def dot_last(a, b):
    return lax.dot_general(a, b, (((1,), (1,)), ((), ())), preferred_element_type=F32)


def dot_first(a, b):
    return lax.dot_general(a, b, (((0,), (0,)), ((), ())), preferred_element_type=F32)


def gelu(x):
    slope = math.sqrt(2.0 / math.pi)
    bend = jnp.tanh(x * (x * x * (0.044715 * slope) + slope))
    half = 0.5 * x
    return half * bend + half


class Gather:
    def __init__(self, n, buf, ssem, rsem):
        me = lax.axis_index("seq")
        self.me, self.n, self.high = me, n, n // 4
        self.buf, self.ssem, self.rsem = buf, ssem, rsem
        self.b0, self.b1, self.hi = me % 2, (me // 2) % 2, me // 4
        self.peer1 = self.hi * 4 + (1 - self.b1) * 2 + self.b0
        self.peer0 = self.hi * 4 + self.b1 * 2 + (1 - self.b0)

    def slot(self, d, b1, b0):
        return ((self.hi + self.high - d) % self.high) * 4 + b1 * 2 + b0

    def copy(self, slot, peer, k):
        return pltpu.make_async_remote_copy(
            src_ref=self.buf.at[slot],
            dst_ref=self.buf.at[slot],
            send_sem=self.ssem.at[k],
            recv_sem=self.rsem.at[slot],
            device_id={"seq": peer},
            device_id_type=MESH,
        )

    def peers(self):
        out = [((self.hi + d) % self.high) * 4 + self.b1 * 2 + self.b0 for d in range(1, self.high)]
        return out + [self.peer1, self.peer0]

    def start(self):
        h = self.high
        for d in range(1, h):
            peer = ((self.hi + d) % h) * 4 + self.b1 * 2 + self.b0
            self.copy(self.me, peer, d - 1).start()
        self.copy(self.me, self.peer1, h - 1).start()
        self.copy(self.me, self.peer0, 2 * h - 1).start()

    def second(self, d):
        h = self.high
        slot = self.slot(d, self.b1, self.b0)
        self.copy(slot, self.peer1, h - 1 + d).wait_recv()
        self.copy(slot, self.peer1, h - 1 + d).start()
        self.copy(slot, self.peer0, 2 * h - 1 + d).start()

    def third(self, d):
        slot = self.slot(d, 1 - self.b1, self.b0)
        self.copy(slot, self.peer0, 3 * self.high - 1 + d).wait_recv()
        self.copy(slot, self.peer0, 3 * self.high - 1 + d).start()

    def finish(self):
        h = self.high
        for b1 in (self.b1, 1 - self.b1):
            for d in range(h):
                slot = self.slot(d, b1, 1 - self.b0)
                self.copy(slot, self.peer0, 0).wait_recv()
        for k in range(4 * h - 1):
            self.copy(self.me, self.peer0, k).wait_send()


def head_column(offset_ref, heads, picked):
    rows = iota((heads * picked, 1), 0) // picked
    column = jnp.zeros((heads * picked, 1), jnp.int32)
    for h in range(heads):
        column = jnp.where(rows == h, offset_ref[h], column)
    return column


def kernel(
    n, heads, picked, stride,
    seg_hbm, glob_hbm, x_hbm, gain1_hbm, gain_mlp_hbm, gain2_hbm,
    wq1_hbm, wk1_hbm, wv1_hbm, wo1_hbm, up_hbm, down_hbm, wq2_hbm, wk2_hbm, wv2_hbm, wo2_hbm,
    out_ref,
    seg_ref, glob_ref, x_ref, gain1_ref, gain_mlp_ref, gain2_ref,
    wq1, wk1, wv1, wo1, up, down, wq2, wk2, wv2, wo2,
    xp, q, kv1, kv2, km, vt, perm, perm_back, mix, mix_odd, sem,
    ssem1, rsem1, ssem2, rsem2,
):
    tokens, width = x_ref.shape
    size = width // heads
    half = LANES // 2
    chunk = heads * picked
    chunks = tokens // chunk
    keys = n * picked
    group = WINDOW // stride
    scale = size ** -0.5 * math.log2(math.e)

    pairs = [(wk1_hbm, wk1), (wv1_hbm, wv1), (wq1_hbm, wq1), (wo1_hbm, wo1), (up_hbm, up),
             (down_hbm, down), (wk2_hbm, wk2), (wv2_hbm, wv2), (wq2_hbm, wq2), (wo2_hbm, wo2),
             (seg_hbm, seg_ref), (x_hbm, x_ref), (gain1_hbm, gain1_ref), (glob_hbm, glob_ref),
             (gain_mlp_hbm, gain_mlp_ref), (gain2_hbm, gain2_ref)]
    loads = [pltpu.make_async_copy(a, b, sem.at[i]) for i, (a, b) in enumerate(pairs)]
    early = (10, 11, 12, 13, 14, 15, 0, 1)
    for i in early:
        loads[i].start()

    first_gather = Gather(n, kv1, ssem1, rsem1)
    second_gather = Gather(n, kv2, ssem2, rsem2)
    barrier = pltpu.get_barrier_semaphore()
    peers = first_gather.peers()
    for peer in peers:
        pl.semaphore_signal(barrier, inc=1, device_id={"seq": peer}, device_id_type=MESH)

    def own_heads(hidden, weight):
        blocks = []
        for start in range(0, width, WINDOW):
            low, top = start // size, -(-(start + WINDOW) // size)
            full = dot32(hidden[low * picked:top * picked], weight[:, start:start + WINDOW])
            column = iota((picked, WINDOW), 1) + start
            total = jnp.zeros((picked, WINDOW), F32)
            for h in range(low, top):
                mine = (column >= h * size) & (column < h * size + size)
                at = (h - low) * picked
                total = jnp.where(mine, full[at:at + picked], total)
            blocks.append(total)
        return jnp.concatenate(blocks, axis=1).astype(BF16)

    rows = iota((chunk, 1), 0)
    pick = rows % picked
    loads[10].wait()
    target = pick * stride + head_column(seg_ref, heads, picked)
    onehot = (iota((chunk, tokens), 1) == target).astype(F32).astype(BF16)
    loads[11].wait()
    loads[12].wait()
    for i in range(2, 10):
        loads[i].start()
    hidden = norm_rows(dot32(onehot, x_ref[...]), gain1_ref[...][None, :])
    me = first_gather.me
    loads[0].wait()
    kv1[me, 0:picked, :] = own_heads(hidden, wk1)
    loads[1].wait()
    kv1[me, picked:2 * picked, :] = own_heads(hidden, wv1)
    pl.semaphore_wait(barrier, len(peers))
    first_gather.start()

    for i in (13, 14, 15):
        loads[i].wait()
    glob_col = head_column(glob_ref, heads, picked)
    lane = iota((16, WINDOW), 1)
    inside = lane % stride
    chosen = jnp.zeros((16, WINDOW), F32)
    for h in range(heads):
        chosen = jnp.where(inside == glob_ref[h], 1.0, chosen)
    a, b = iota((WINDOW, WINDOW), 0), iota((WINDOW, WINDOW), 1)
    same = a // stride == b // stride
    before = jnp.where(same & (a < b), 1.0, 0.0).astype(BF16)
    count = dot32(chosen.astype(BF16), before)
    total = dot32(chosen.astype(BF16), jnp.where(same, 1.0, 0.0).astype(BF16))
    rank = jnp.where(chosen > 0.5, count, total + inside.astype(F32) - count)
    rank_row = rank[0:1, :]
    table = jnp.where(same & (rank_row == (a % stride).astype(F32)), 1.0, 0.0)
    perm[...] = table.astype(BF16)
    perm_back[...] = table.T.astype(BF16)
    at_head = (iota((chunk, WINDOW), 1) == glob_col)
    head_rank = jnp.sum(jnp.where(at_head, rank_row, 0.0), axis=1, keepdims=True)
    spot = (pick * heads).astype(F32) + head_rank
    onehot_two = (iota((chunk, chunk), 1).astype(F32) == spot).astype(F32).astype(BF16)

    for g in range(tokens // WINDOW):
        moved = dot32(perm[...], x_ref[g * WINDOW:(g + 1) * WINDOW, :]).astype(BF16)
        for j in range(group):
            for c in range(chunks):
                at = c * chunk + (g * group + j) * heads
                xp[at:at + heads, :] = moved[j * stride + c * heads:j * stride + (c + 1) * heads]

    def window_of(h):
        return min(h * size // LANES * LANES, width - WINDOW)

    for h in range(heads):
        km[h] = jnp.zeros((WINDOW, keys), BF16)
        vt[h * half + size:(h + 1) * half, :] = jnp.ones((half - size, keys), BF16)

    loads[2].wait()
    loads[3].wait()
    high = first_gather.high

    def query_chunk(c, carry):
        at = pl.ds(pl.multiple_of(c * chunk, chunk), chunk)
        hidden = norm_rows(xp[at, :].astype(F32), gain1_ref[...][None, :])
        q[at, :] = dot32(hidden, wq1[...]).astype(BF16)
        for d in range(1, high):
            @pl.when(c == d - 1)
            def _(d=d):
                first_gather.second(d)

        return carry

    lax.fori_loop(0, chunks, query_chunk, 0)
    for d in range(high):
        first_gather.third(d)
    first_gather.finish()

    def set_keys(kv, first, last):
        span = (last - first) * size
        key = kv[:, 0:picked, :].reshape(keys, span).astype(F32).T.astype(BF16)
        value = kv[:, picked:2 * picked, :].reshape(keys, span).astype(F32).T.astype(BF16)
        for h in range(first, last):
            begin = h * size - window_of(h)
            at = (h - first) * size
            km[h, begin:begin + size, :] = key[at:at + size, :]
            vt[h * half:h * half + size, :] = value[at:at + size, :]

    def attend(at, mix):
        def score(h):
            start = window_of(h)
            return dot32(q[at, start:start + WINDOW], km[h])

        def soften(scores):
            top = jnp.max(scores, axis=-1, keepdims=True)
            return jnp.exp2((scores - top) * scale).astype(BF16)

        def blend(h, weights):
            both = dot_last(vt[h * half:(h + 1) * half, :], weights)
            mixed = both[:size] * (1.0 / both[size:size + 1])
            mix[h * size:(h + 1) * size, :] = mixed.astype(BF16)

        steps = heads // GROUP
        scores, weights = {}, {}
        for i in range(steps + 2):
            if i < steps:
                for h in range(i * GROUP, (i + 1) * GROUP):
                    scores[h] = score(h)
            if 1 <= i <= steps:
                for h in range((i - 1) * GROUP, i * GROUP):
                    weights[h] = soften(scores.pop(h))
            if i >= 2:
                for h in range((i - 2) * GROUP, (i - 1) * GROUP):
                    blend(h, weights.pop(h))
            yield i

    def rows_of(c):
        return pl.ds(pl.multiple_of(c * chunk, chunk), chunk)

    set_keys(kv1, 0, heads)
    loads[4].wait()
    loads[5].wait()
    loads[6].wait()
    loads[7].wait()
    loads[8].wait()

    for _ in attend(rows_of(0), mix):
        pass

    def first_chunk(c, more):
        at = rows_of(c)
        first = (xp[at, :].astype(F32) + dot_first(mix[...], wo1[...])).astype(BF16)
        total = first.astype(F32)
        normed = norm_rows(total, gain_mlp_ref[...][None, :])
        blocks = up.shape[1] // WINDOW
        units = {}
        ahead = attend(rows_of(c + 1), mix) if more else iter(())
        for j in range(blocks + 1):
            next(ahead, None)
            if j < blocks:
                part = dot32(normed, up[:, j * WINDOW:(j + 1) * WINDOW])
                units[j] = gelu(part).astype(BF16)
            if j >= 1:
                total = total + dot32(units.pop(j - 1), down[(j - 1) * WINDOW:j * WINDOW, :])
        for _ in ahead:
            pass
        second = total.astype(BF16)
        xp[at, :] = second
        hidden_two = norm_rows(second.astype(F32), gain2_ref[...][None, :])
        q[at, :] = dot32(hidden_two, wq2[...]).astype(BF16)

        return hidden_two

    def first_step(c, carry):
        hidden_two = first_chunk(c, True)

        @pl.when(c == 0)
        def _():
            picked_rows = dot32(onehot_two, hidden_two).astype(BF16)
            kv2[me, 0:picked, :] = own_heads(picked_rows, wk2)
            kv2[me, picked:2 * picked, :] = own_heads(picked_rows, wv2)
            second_gather.start()

        @pl.when(c == 1)
        def _():
            for d in range(1, high):
                second_gather.second(d)

        @pl.when(c == 2)
        def _():
            for d in range(high):
                second_gather.third(d)

        return carry

    lax.fori_loop(0, chunks - 1, first_step, 0)
    first_chunk(chunks - 1, False)
    loads[9].wait()
    second_gather.finish()
    set_keys(kv2, 0, heads)

    def project(c):
        at = rows_of(c)
        for start in range(0, width, WINDOW):
            part = dot_first(mixes[c % 2][...], wo2[:, start:start + WINDOW])
            column = slice(start, start + WINDOW)
            xp[at, column] = (xp[at, column].astype(F32) + part).astype(BF16)
            yield start

    mixes = (mix, mix_odd)
    behind = iter(())
    for c in range(chunks):
        for i in attend(rows_of(c), mixes[c % 2]):
            if i >= 1:
                next(behind, None)
        for _ in behind:
            pass
        behind = project(c)
    for _ in behind:
        pass
    for g in range(tokens // WINDOW):
        blocks = []
        for j in range(group):
            for c in range(chunks):
                at = c * chunk + (g * group + j) * heads
                blocks.append(xp[at:at + heads, :])
        moved = dot32(perm_back[...], jnp.concatenate(blocks, axis=0))
        out_ref[g * WINDOW:(g + 1) * WINDOW, :] = moved.astype(BF16)


def whole_body(
    tokens, attn_gain, query_first, key_first, segment_value, output_first, mlp_gain, up_weight,
    down_weight, second_gain, query_second, key_second, value_second, output_second,
    segment_offset, global_offset,
):
    n = lax.axis_size("seq")
    heads = segment_offset.shape[0]
    picked = KEYS // n
    count, width = tokens.shape
    stride = count // picked
    units = up_weight.shape[1]
    chunk = heads * picked
    outside = pl.BlockSpec(memory_space=pltpu.HBM)
    vmem = pl.BlockSpec(memory_space=pltpu.VMEM)
    square = pltpu.VMEM((width, width), BF16)
    gain = pltpu.VMEM((width,), F32)
    shared = pltpu.VMEM((n, 2 * picked, width), BF16)
    links = pltpu.SemaphoreType.DMA((n,))
    return pl.pallas_call(
        functools.partial(kernel, n, heads, picked, stride),
        out_shape=jax.ShapeDtypeStruct(tokens.shape, tokens.dtype),
        in_specs=[outside] * 16,
        out_specs=vmem,
        scratch_shapes=[
            pltpu.SMEM((heads,), jnp.int32), pltpu.SMEM((heads,), jnp.int32),
            pltpu.VMEM((count, width), BF16),
            gain, gain, gain,
            square, square, square, square,
            pltpu.VMEM((width, units), BF16), pltpu.VMEM((units, width), BF16),
            square, square, square, square,
            pltpu.VMEM((count, width), BF16),
            pltpu.VMEM((count, width), BF16),
            shared, shared,
            pltpu.VMEM((heads, WINDOW, KEYS), BF16),
            pltpu.VMEM((heads * LANES // 2, KEYS), BF16),
            pltpu.VMEM((WINDOW, WINDOW), BF16),
            pltpu.VMEM((WINDOW, WINDOW), BF16),
            pltpu.VMEM((width, chunk), BF16),
            pltpu.VMEM((width, chunk), BF16),
            pltpu.SemaphoreType.DMA((16,)),
            links, links, links, links,
        ],
        compiler_params=pltpu.CompilerParams(
            collective_id=0, has_side_effects=True, vmem_limit_bytes=60 << 20
        ),
        name="encoder",
    )(
        segment_offset, global_offset, tokens, attn_gain, mlp_gain, second_gain,
        query_first, key_first, segment_value, output_first, up_weight, down_weight,
        query_second, key_second, value_second, output_second,
    )


def fits(mesh):
    n = mesh.shape["seq"]
    return mesh.shape["mp"] == 1 and n == SEG_MAX


def choose(mesh):
    return whole_body if fits(mesh) else body


def solution(mesh):
    placed = (
        P(("slides", "seq", "mp"), None),
        P(),
        P(None, "mp"),
        P(None, "mp"),
        P(None, "mp"),
        P("mp", None),
        P(),
        P(None, "mp"),
        P("mp", None),
        P(),
        P(None, "mp"),
        P(None, "mp"),
        P(None, "mp"),
        P("mp", None),
        P("mp"),
        P("mp"),
    )
    return jax.shard_map(
        choose(mesh),
        mesh=mesh,
        in_specs=placed,
        out_specs=P(("slides", "seq", "mp"), None),
        check_vma=False,
    )
```

```python
import functools
import math

import jax
import jax.numpy as jnp
from jax import lax
from jax.experimental import pallas as pl
from jax.experimental.pallas import tpu as pltpu
from jax.sharding import PartitionSpec as P

KEYS = 256
SEG_MAX = 16


def swapped(x, axis, apart):
    return lax.ppermute(x, axis, [(i, i ^ 1 << apart) for i in range(lax.axis_size(axis))])


def norm_rows(values, gain):
    center = values - jnp.mean(values, axis=-1, keepdims=True)
    spread = jnp.mean(center * center, axis=-1, keepdims=True)
    return (center * lax.rsqrt(spread + 1e-05) * gain).astype(jnp.bfloat16)


def pick_keys(hidden, offsets, stride, key_weight, value_weight):
    token_count, width = hidden.shape
    head_count = offsets.shape[0]
    head_size = key_weight.shape[1] // head_count
    grouped_rows = hidden.reshape(token_count // stride, stride, width)
    dilation_selector = (
        lax.broadcasted_iota(jnp.int32, (stride, head_count), 0) == offsets[None, :]
    ).astype(jnp.bfloat16)
    chosen = jnp.einsum(
        "nof,oj->njf", grouped_rows, dilation_selector, preferred_element_type=jnp.float32
    ).astype(jnp.bfloat16)
    key_heads = jnp.einsum(
        "xkr,rkf->xkf",
        chosen,
        key_weight.reshape(width, head_count, head_size),
        preferred_element_type=jnp.float32,
    ).astype(jnp.bfloat16)
    value_heads = jnp.einsum(
        "xkr,rkf->xkf",
        chosen,
        value_weight.reshape(width, head_count, head_size),
        preferred_element_type=jnp.float32,
    ).astype(jnp.bfloat16)
    picked = token_count // stride
    return jnp.stack(
        [
            key_heads.reshape(picked, head_count * head_size),
            value_heads.reshape(picked, head_count * head_size),
        ]
    )


def attend_local(query, keyval, head_count):
    token_count, width = query.shape
    head_size = width // head_count
    query_heads = query.reshape(token_count, head_count, head_size)
    key_heads = keyval[0].reshape(-1, head_count, head_size)
    value_heads = keyval[1].reshape(-1, head_count, head_size)
    scores = jnp.einsum(
        "thd,khd->htk", query_heads, key_heads, preferred_element_type=jnp.float32
    ) * head_size ** (-0.5)
    highest = jnp.max(scores, axis=-1, keepdims=True)
    weights = jnp.exp(scores - highest)
    weights = (weights / jnp.sum(weights, axis=-1, keepdims=True)).astype(jnp.bfloat16)
    mixed = jnp.einsum(
        "htk,khd->thd", weights, value_heads, preferred_element_type=jnp.float32
    ).astype(jnp.bfloat16)
    return mixed.reshape(token_count, width)


def merge_branch_pair(mine, other, level, token_position):
    lower = token_position >> level & 1 == 0
    return jnp.where(
        lower, jnp.concatenate((mine, other), axis=1), jnp.concatenate((other, mine), axis=1)
    )


def spread_segment(keyval, seg_span, token_position):
    for level in range(seg_span.bit_length() - 1):
        partner = swapped(keyval, "seq", level)
        keyval = merge_branch_pair(keyval, partner, level, token_position)
    return keyval


def spread_global(keyval_two):
    keyval_two = lax.all_gather(keyval_two, "seq", axis=1, tiled=True)
    return keyval_two


def combine(partial_value, residual_full, need_full):
    row_count = residual_full.shape[0] // lax.axis_size("mp")
    row_start = lax.axis_index("mp") * row_count
    share = lax.psum_scatter(partial_value, "mp", scatter_dimension=0, tiled=True)
    own_rows = lax.dynamic_slice_in_dim(residual_full, row_start, row_count, 0)
    own_rows = (own_rows.astype(jnp.float32) + share).astype(jnp.bfloat16)
    full_rows = lax.all_gather(own_rows, "mp", axis=0, tiled=True) if need_full else own_rows
    return (own_rows, full_rows)


def body(
    tokens,
    attn_gain,
    query_first,
    key_first,
    segment_value,
    output_first,
    mlp_gain,
    up_weight,
    down_weight,
    second_gain,
    query_second,
    key_second,
    value_second,
    output_second,
    segment_offset,
    global_offset,
):
    seq_count = lax.axis_size("seq")
    token_position = lax.axis_index("seq")
    seg_span = min(SEG_MAX, seq_count)
    head_count = segment_offset.shape[0]
    full_rows = lax.all_gather(tokens, "mp", axis=0, tiled=True)
    token_count = full_rows.shape[0]
    hidden = norm_rows(full_rows.astype(jnp.float32), attn_gain)
    query = jnp.dot(hidden, query_first, preferred_element_type=jnp.float32).astype(jnp.bfloat16)
    seg_stride = token_count // (KEYS // seg_span)
    keyval = pick_keys(hidden, segment_offset, seg_stride, key_first, segment_value)
    keyval = spread_segment(keyval, seg_span, token_position)
    mixed = attend_local(query, keyval, head_count)
    partial_value = jnp.dot(mixed, output_first, preferred_element_type=jnp.float32)
    own_rows, first_rows = combine(partial_value, full_rows, True)
    normed = norm_rows(first_rows.astype(jnp.float32), mlp_gain)
    inner = jax.nn.gelu(
        jnp.dot(normed, up_weight, preferred_element_type=jnp.float32), approximate=True
    ).astype(jnp.bfloat16)
    partial_value = jnp.dot(inner, down_weight, preferred_element_type=jnp.float32)
    own_rows, second_rows = combine(partial_value, first_rows, True)
    hidden_two = norm_rows(second_rows.astype(jnp.float32), second_gain)
    query_two = jnp.dot(hidden_two, query_second, preferred_element_type=jnp.float32).astype(
        jnp.bfloat16
    )
    glob_stride = token_count // (KEYS // seq_count)
    keyval_two = pick_keys(hidden_two, global_offset, glob_stride, key_second, value_second)
    keyval_two = spread_global(keyval_two)
    mixed_two = attend_local(query_two, keyval_two, head_count)
    partial_value = jnp.dot(mixed_two, output_second, preferred_element_type=jnp.float32)
    own_rows, unused_rows = combine(partial_value, second_rows, False)
    return own_rows


MESH = pl.DeviceIdType.MESH
F32 = jnp.float32
BF16 = jnp.bfloat16
WINDOW = 256
LANES = 128
GROUP = 2


def iota(shape, axis):
    return lax.broadcasted_iota(jnp.int32, shape, axis)


def dot32(a, b):
    return jnp.dot(a, b, preferred_element_type=F32)


def dot_last(a, b):
    return lax.dot_general(a, b, (((1,), (1,)), ((), ())), preferred_element_type=F32)


def dot_first(a, b):
    return lax.dot_general(a, b, (((0,), (0,)), ((), ())), preferred_element_type=F32)


def gelu(x):
    slope = math.sqrt(2.0 / math.pi)
    bend = jnp.tanh(x * (x * x * (0.044715 * slope) + slope))
    half = 0.5 * x
    return half * bend + half


class Gather:
    def __init__(self, n, buf, ssem, rsem):
        me = lax.axis_index("seq")
        self.me, self.n, self.high = me, n, n // 4
        self.buf, self.ssem, self.rsem = buf, ssem, rsem
        self.b0, self.b1, self.hi = me % 2, (me // 2) % 2, me // 4
        self.peer1 = self.hi * 4 + (1 - self.b1) * 2 + self.b0
        self.peer0 = self.hi * 4 + self.b1 * 2 + (1 - self.b0)

    def slot(self, d, b1, b0):
        return ((self.hi + self.high - d) % self.high) * 4 + b1 * 2 + b0

    def copy(self, slot, peer, k):
        return pltpu.make_async_remote_copy(
            src_ref=self.buf.at[slot],
            dst_ref=self.buf.at[slot],
            send_sem=self.ssem.at[k],
            recv_sem=self.rsem.at[slot],
            device_id={"seq": peer},
            device_id_type=MESH,
        )

    def far(self, d):
        return ((self.hi + d) % self.high) * 4 + self.b1 * 2 + self.b0

    def peers(self):
        out = [((self.hi + d) % self.high) * 4 + self.b1 * 2 + self.b0 for d in range(1, self.high)]
        return out + [self.peer1, self.peer0]

    def start(self):
        h = self.high
        for d in range(1, h):
            peer = ((self.hi + d) % h) * 4 + self.b1 * 2 + self.b0
            self.copy(self.me, peer, d - 1).start()
        self.copy(self.me, self.peer1, h - 1).start()
        self.copy(self.me, self.peer0, 2 * h - 1).start()

    def second(self, d):
        h = self.high
        slot = self.slot(d, self.b1, self.b0)
        self.copy(slot, self.peer1, h - 1 + d).wait_recv()
        self.copy(slot, self.peer1, h - 1 + d).start()
        self.copy(slot, self.peer0, 2 * h - 1 + d).start()

    def start_across(self):
        self.copy(self.me, self.peer1, 0).start()
        self.copy(self.me, self.peer0, 1).start()
        for d in range(1, self.high):
            self.copy(self.me, self.far(d), 1 + d).start()

    def turn(self):
        slot = self.peer1
        self.copy(slot, self.peer0, 2 * self.high).wait_recv()
        for d in range(1, self.high):
            self.copy(slot, self.far(d), self.high + d).start()
        self.copy(slot, self.peer0, 2 * self.high).start()

    def relay(self, d, b1, k):
        slot = self.slot(d, b1, self.b0)
        self.copy(slot, self.peer0, k).wait_recv()
        self.copy(slot, self.peer0, k).start()

    def third(self, d):
        slot = self.slot(d, 1 - self.b1, self.b0)
        self.copy(slot, self.peer0, 3 * self.high - 1 + d).wait_recv()
        self.copy(slot, self.peer0, 3 * self.high - 1 + d).start()

    def finish(self):
        h = self.high
        for b1 in (self.b1, 1 - self.b1):
            for d in range(h):
                slot = self.slot(d, b1, 1 - self.b0)
                self.copy(slot, self.peer0, 0).wait_recv()
        for k in range(4 * h - 1):
            self.copy(self.me, self.peer0, k).wait_send()


def head_column(offset_ref, heads, picked):
    rows = iota((heads * picked, 1), 0) // picked
    column = jnp.zeros((heads * picked, 1), jnp.int32)
    for h in range(heads):
        column = jnp.where(rows == h, offset_ref[h], column)
    return column


def kernel(
    n, heads, picked, stride,
    seg_hbm, glob_hbm, x_hbm, gain1_hbm, gain_mlp_hbm, gain2_hbm,
    wq1_hbm, wk1_hbm, wv1_hbm, wo1_hbm, up_hbm, down_hbm, wq2_hbm, wk2_hbm, wv2_hbm, wo2_hbm,
    out_ref,
    seg_ref, glob_ref, x_ref, gain1_ref, gain_mlp_ref, gain2_ref,
    wq1, wk1, wv1, wo1, up, down, wq2, wk2, wv2, wo2,
    xp, q, q_two, normed, key1, value1, kv2, km, vt, perm, perm_back, mix, mix_odd, sem,
    ssemk, rsemk, ssemv, rsemv, ssem2, rsem2,
):
    tokens, width = x_ref.shape
    size = width // heads
    half = LANES // 2
    chunk = heads * picked
    chunks = tokens // chunk
    keys = n * picked
    group = WINDOW // stride
    scale = size ** -0.5 * math.log2(math.e)

    pairs = [(wk1_hbm, wk1), (wv1_hbm, wv1), (wq1_hbm, wq1), (wo1_hbm, wo1), (up_hbm, up),
             (down_hbm, down), (wk2_hbm, wk2), (wv2_hbm, wv2), (wq2_hbm, wq2), (wo2_hbm, wo2),
             (seg_hbm, seg_ref), (x_hbm, x_ref), (gain1_hbm, gain1_ref), (glob_hbm, glob_ref),
             (gain_mlp_hbm, gain_mlp_ref), (gain2_hbm, gain2_ref)]
    loads = [pltpu.make_async_copy(a, b, sem.at[i]) for i, (a, b) in enumerate(pairs)]
    early = (10, 11, 12, 13, 14, 15, 0, 1)
    for i in early:
        loads[i].start()

    key_gather = Gather(n, key1, ssemk, rsemk)
    value_gather = Gather(n, value1, ssemv, rsemv)
    second_gather = Gather(n, kv2, ssem2, rsem2)
    barrier = pltpu.get_barrier_semaphore()
    peers = key_gather.peers()
    for peer in peers:
        pl.semaphore_signal(barrier, inc=1, device_id={"seq": peer}, device_id_type=MESH)

    def own_heads(hidden, weight):
        blocks = []
        for start in range(0, width, WINDOW):
            low, top = start // size, -(-(start + WINDOW) // size)
            full = dot32(hidden[low * picked:top * picked], weight[:, start:start + WINDOW])
            column = iota((picked, WINDOW), 1) + start
            total = jnp.zeros((picked, WINDOW), F32)
            for h in range(low, top):
                mine = (column >= h * size) & (column < h * size + size)
                at = (h - low) * picked
                total = jnp.where(mine, full[at:at + picked], total)
            blocks.append(total)
        return jnp.concatenate(blocks, axis=1).astype(BF16)

    rows = iota((chunk, 1), 0)
    pick = rows % picked
    loads[10].wait()
    target = pick * stride + head_column(seg_ref, heads, picked)
    onehot = (iota((chunk, tokens), 1) == target).astype(F32).astype(BF16)
    loads[11].wait()
    loads[12].wait()
    for i in range(2, 10):
        loads[i].start()
    hidden = norm_rows(dot32(onehot, x_ref[...]), gain1_ref[...][None, :])
    me = key_gather.me
    loads[0].wait()
    key1[me] = own_heads(hidden, wk1)
    pl.semaphore_wait(barrier, len(peers))
    key_gather.start()
    loads[1].wait()
    value1[me] = own_heads(hidden, wv1)
    value_gather.start_across()

    for i in (13, 14, 15):
        loads[i].wait()
    glob_col = head_column(glob_ref, heads, picked)
    lane = iota((16, WINDOW), 1)
    inside = lane % stride
    chosen = jnp.zeros((16, WINDOW), F32)
    for h in range(heads):
        chosen = jnp.where(inside == glob_ref[h], 1.0, chosen)
    a, b = iota((WINDOW, WINDOW), 0), iota((WINDOW, WINDOW), 1)
    same = a // stride == b // stride
    before = jnp.where(same & (a < b), 1.0, 0.0).astype(BF16)
    count = dot32(chosen.astype(BF16), before)
    total = dot32(chosen.astype(BF16), jnp.where(same, 1.0, 0.0).astype(BF16))
    rank = jnp.where(chosen > 0.5, count, total + inside.astype(F32) - count)
    rank_row = rank[0:1, :]
    table = jnp.where(same & (rank_row == (a % stride).astype(F32)), 1.0, 0.0)
    perm[...] = table.astype(BF16)
    perm_back[...] = table.T.astype(BF16)
    at_head = (iota((chunk, WINDOW), 1) == glob_col)
    head_rank = jnp.sum(jnp.where(at_head, rank_row, 0.0), axis=1, keepdims=True)
    spot = (pick * heads).astype(F32) + head_rank
    onehot_two = (iota((chunk, chunk), 1).astype(F32) == spot).astype(F32).astype(BF16)

    for g in range(tokens // WINDOW):
        moved = dot32(perm[...], x_ref[g * WINDOW:(g + 1) * WINDOW, :]).astype(BF16)
        for j in range(group):
            for c in range(chunks):
                at = c * chunk + (g * group + j) * heads
                xp[at:at + heads, :] = moved[j * stride + c * heads:j * stride + (c + 1) * heads]

    def window_of(h):
        return min(h * size // LANES * LANES, width - WINDOW)

    for h in range(heads):
        km[h] = jnp.zeros((WINDOW, keys), BF16)
        vt[h * half + size:(h + 1) * half, :] = jnp.ones((half - size, keys), BF16)

    loads[2].wait()
    loads[3].wait()
    high = key_gather.high

    def query_chunk(c, carry):
        at = pl.ds(pl.multiple_of(c * chunk, chunk), chunk)
        hidden = norm_rows(xp[at, :].astype(F32), gain1_ref[...][None, :])
        q[at, :] = dot32(hidden, wq1[...]).astype(BF16)
        @pl.when(c == 0)
        def _():
            value_gather.turn()

        for d in range(1, high):
            @pl.when(c == d)
            def _(d=d):
                key_gather.second(d)

        return carry

    lax.fori_loop(0, chunks, query_chunk, 0)
    key_gather.third(0)
    for d in range(1, high):
        value_gather.relay(d, value_gather.b1, 2 * high + d)
        key_gather.third(d)
    for d in range(1, high):
        value_gather.relay(d, 1 - value_gather.b1, 3 * high - 1 + d)
    key_gather.finish()
    value_gather.finish()

    def set_keys(key, value):
        key = key.reshape(keys, width).astype(F32).T.astype(BF16)
        value = value.reshape(keys, width).astype(F32).T.astype(BF16)
        for h in range(heads):
            begin = h * size - window_of(h)
            at = h * size
            km[h, begin:begin + size, :] = key[at:at + size, :]
            vt[h * half:h * half + size, :] = value[at:at + size, :]

    def attend(at, q, mix):
        def score(h):
            start = window_of(h)
            return dot32(q[at, start:start + WINDOW], km[h])

        def soften(scores):
            top = jnp.max(scores, axis=-1, keepdims=True)
            return jnp.exp2((scores - top) * scale).astype(BF16)

        def blend(h, weights):
            both = dot_last(vt[h * half:(h + 1) * half, :], weights)
            mixed = both[:size] * (1.0 / both[size:size + 1])
            mix[h * size:(h + 1) * size, :] = mixed.astype(BF16)

        steps = heads // GROUP
        scores, weights = {}, {}
        for i in range(steps + 2):
            if i < steps:
                for h in range(i * GROUP, (i + 1) * GROUP):
                    scores[h] = score(h)
            if 1 <= i <= steps:
                for h in range((i - 1) * GROUP, i * GROUP):
                    weights[h] = soften(scores.pop(h))
            if i >= 2:
                for h in range((i - 2) * GROUP, (i - 1) * GROUP):
                    blend(h, weights.pop(h))
            yield i

    def rows_of(c):
        return pl.ds(pl.multiple_of(c * chunk, chunk), chunk)

    set_keys(key1[...], value1[...])
    loads[4].wait()
    loads[5].wait()
    loads[6].wait()
    loads[7].wait()
    loads[8].wait()

    def query_two(c):
        at = rows_of(c)
        hidden_two = norm_rows(xp[at, :].astype(F32), gain2_ref[...][None, :])
        for start in range(0, width, WINDOW):
            column = slice(start, start + WINDOW)
            q_two[at, column] = dot32(hidden_two, wq2[:, column]).astype(BF16)
            yield start

    def enter(c):
        at = rows_of(c)
        parts = []
        for start in range(0, width, WINDOW):
            column = slice(start, start + WINDOW)
            parts.append(xp[at, column].astype(F32) + dot_first(mix[...], wo1[:, column]))
            yield start
        first = jnp.concatenate(parts, axis=1).astype(BF16)
        xp[at, :] = first
        normed[...] = norm_rows(first.astype(F32), gain_mlp_ref[...][None, :])

    def first_chunk(c, more, late):
        at = rows_of(c)
        total = xp[at, :].astype(F32)
        blocks = up.shape[1] // WINDOW
        units = {}
        ahead = attend(rows_of(c + 1), q, mix) if more else iter(())
        behind = query_two(late)
        for j in range(blocks + 1):
            next(ahead, None)
            if j % 3 == 1:
                next(behind, None)
            if j < blocks:
                part = dot32(normed[...], up[:, j * WINDOW:(j + 1) * WINDOW])
                units[j] = gelu(part).astype(BF16)
            if j >= 1:
                total = total + dot32(units.pop(j - 1), down[(j - 1) * WINDOW:j * WINDOW, :])
        for rest in (behind, ahead):
            for _ in rest:
                pass
        second = total.astype(BF16)
        xp[at, :] = second
        if more:
            for _ in enter(c + 1):
                pass
        return second

    for _ in attend(rows_of(0), q, mix):
        pass
    for _ in enter(0):
        pass

    def first_step(c, carry):
        second = first_chunk(c, True, (c + chunks - 1) % chunks)

        @pl.when(c == 0)
        def _():
            rows = dot32(onehot_two, second)
            picked_rows = norm_rows(rows, gain2_ref[...][None, :])
            kv2[me, 0:picked, :] = own_heads(picked_rows, wk2)
            kv2[me, picked:2 * picked, :] = own_heads(picked_rows, wv2)
            second_gather.start()

        @pl.when(c == 1)
        def _():
            for d in range(1, high):
                second_gather.second(d)

        @pl.when(c == 2)
        def _():
            for d in range(high):
                second_gather.third(d)

        return carry

    lax.fori_loop(0, chunks - 1, first_step, 0)
    first_chunk(chunks - 1, False, chunks - 2)
    for _ in query_two(chunks - 1):
        pass
    loads[9].wait()
    second_gather.finish()
    set_keys(kv2[:, 0:picked, :], kv2[:, picked:2 * picked, :])

    def project(c):
        at = rows_of(c)
        for start in range(0, width, WINDOW):
            part = dot_first(mixes[c % 2][...], wo2[:, start:start + WINDOW])
            column = slice(start, start + WINDOW)
            xp[at, column] = (xp[at, column].astype(F32) + part).astype(BF16)
            yield start

    mixes = (mix, mix_odd)
    behind = iter(())
    for c in range(chunks):
        for i in attend(rows_of(c), q_two, mixes[c % 2]):
            if i >= 1:
                next(behind, None)
        for _ in behind:
            pass
        behind = project(c)
    for _ in behind:
        pass
    for g in range(tokens // WINDOW):
        blocks = []
        for j in range(group):
            for c in range(chunks):
                at = c * chunk + (g * group + j) * heads
                blocks.append(xp[at:at + heads, :])
        moved = dot32(perm_back[...], jnp.concatenate(blocks, axis=0))
        out_ref[g * WINDOW:(g + 1) * WINDOW, :] = moved.astype(BF16)


def whole_body(
    tokens, attn_gain, query_first, key_first, segment_value, output_first, mlp_gain, up_weight,
    down_weight, second_gain, query_second, key_second, value_second, output_second,
    segment_offset, global_offset,
):
    n = lax.axis_size("seq")
    heads = segment_offset.shape[0]
    picked = KEYS // n
    count, width = tokens.shape
    stride = count // picked
    units = up_weight.shape[1]
    chunk = heads * picked
    outside = pl.BlockSpec(memory_space=pltpu.HBM)
    vmem = pl.BlockSpec(memory_space=pltpu.VMEM)
    square = pltpu.VMEM((width, width), BF16)
    gain = pltpu.VMEM((width,), F32)
    own = pltpu.VMEM((n, picked, width), BF16)
    links = pltpu.SemaphoreType.DMA((n,))
    return pl.pallas_call(
        functools.partial(kernel, n, heads, picked, stride),
        out_shape=jax.ShapeDtypeStruct(tokens.shape, tokens.dtype),
        in_specs=[outside] * 16,
        out_specs=vmem,
        scratch_shapes=[
            pltpu.SMEM((heads,), jnp.int32), pltpu.SMEM((heads,), jnp.int32),
            pltpu.VMEM((count, width), BF16),
            gain, gain, gain,
            square, square, square, square,
            pltpu.VMEM((width, units), BF16), pltpu.VMEM((units, width), BF16),
            square, square, square, square,
            pltpu.VMEM((count, width), BF16),
            pltpu.VMEM((count, width), BF16),
            pltpu.VMEM((count, width), BF16),
            pltpu.VMEM((chunk, width), BF16),
            own, own,
            pltpu.VMEM((n, 2 * picked, width), BF16),
            pltpu.VMEM((heads, WINDOW, KEYS), BF16),
            pltpu.VMEM((heads * LANES // 2, KEYS), BF16),
            pltpu.VMEM((WINDOW, WINDOW), BF16),
            pltpu.VMEM((WINDOW, WINDOW), BF16),
            pltpu.VMEM((width, chunk), BF16),
            pltpu.VMEM((width, chunk), BF16),
            pltpu.SemaphoreType.DMA((16,)),
            links, links, links, links, links, links,
        ],
        compiler_params=pltpu.CompilerParams(
            collective_id=0, has_side_effects=True, vmem_limit_bytes=60 << 20
        ),
        name="encoder",
    )(
        segment_offset, global_offset, tokens, attn_gain, mlp_gain, second_gain,
        query_first, key_first, segment_value, output_first, up_weight, down_weight,
        query_second, key_second, value_second, output_second,
    )


def fits(mesh):
    n = mesh.shape["seq"]
    return mesh.shape["mp"] == 1 and n == SEG_MAX


def choose(mesh):
    return whole_body if fits(mesh) else body


def solution(mesh):
    placed = (
        P(("slides", "seq", "mp"), None),
        P(),
        P(None, "mp"),
        P(None, "mp"),
        P(None, "mp"),
        P("mp", None),
        P(),
        P(None, "mp"),
        P("mp", None),
        P(),
        P(None, "mp"),
        P(None, "mp"),
        P(None, "mp"),
        P("mp", None),
        P("mp"),
        P("mp"),
    )
    return jax.shard_map(
        choose(mesh),
        mesh=mesh,
        in_specs=placed,
        out_specs=P(("slides", "seq", "mp"), None),
        check_vma=False,
    )
```

```python
import functools
import math

import jax
import jax.numpy as jnp
from jax import lax
from jax.experimental import pallas as pl
from jax.experimental.pallas import tpu as pltpu
from jax.sharding import PartitionSpec as P

KEYS = 256
SEG_MAX = 16


def swapped(x, axis, apart):
    return lax.ppermute(x, axis, [(i, i ^ 1 << apart) for i in range(lax.axis_size(axis))])


def norm_rows(values, gain):
    center = values - jnp.mean(values, axis=-1, keepdims=True)
    spread = jnp.mean(center * center, axis=-1, keepdims=True)
    return (center * lax.rsqrt(spread + 1e-05) * gain).astype(jnp.bfloat16)


def pick_keys(hidden, offsets, stride, key_weight, value_weight):
    token_count, width = hidden.shape
    head_count = offsets.shape[0]
    head_size = key_weight.shape[1] // head_count
    grouped_rows = hidden.reshape(token_count // stride, stride, width)
    dilation_selector = (
        lax.broadcasted_iota(jnp.int32, (stride, head_count), 0) == offsets[None, :]
    ).astype(jnp.bfloat16)
    chosen = jnp.einsum(
        "nof,oj->njf", grouped_rows, dilation_selector, preferred_element_type=jnp.float32
    ).astype(jnp.bfloat16)
    key_heads = jnp.einsum(
        "xkr,rkf->xkf",
        chosen,
        key_weight.reshape(width, head_count, head_size),
        preferred_element_type=jnp.float32,
    ).astype(jnp.bfloat16)
    value_heads = jnp.einsum(
        "xkr,rkf->xkf",
        chosen,
        value_weight.reshape(width, head_count, head_size),
        preferred_element_type=jnp.float32,
    ).astype(jnp.bfloat16)
    picked = token_count // stride
    return jnp.stack(
        [
            key_heads.reshape(picked, head_count * head_size),
            value_heads.reshape(picked, head_count * head_size),
        ]
    )


def attend_local(query, keyval, head_count):
    token_count, width = query.shape
    head_size = width // head_count
    query_heads = query.reshape(token_count, head_count, head_size)
    key_heads = keyval[0].reshape(-1, head_count, head_size)
    value_heads = keyval[1].reshape(-1, head_count, head_size)
    scores = jnp.einsum(
        "thd,khd->htk", query_heads, key_heads, preferred_element_type=jnp.float32
    ) * head_size ** (-0.5)
    highest = jnp.max(scores, axis=-1, keepdims=True)
    weights = jnp.exp(scores - highest)
    weights = (weights / jnp.sum(weights, axis=-1, keepdims=True)).astype(jnp.bfloat16)
    mixed = jnp.einsum(
        "htk,khd->thd", weights, value_heads, preferred_element_type=jnp.float32
    ).astype(jnp.bfloat16)
    return mixed.reshape(token_count, width)


def merge_branch_pair(mine, other, level, token_position):
    lower = token_position >> level & 1 == 0
    return jnp.where(
        lower, jnp.concatenate((mine, other), axis=1), jnp.concatenate((other, mine), axis=1)
    )


def spread_segment(keyval, seg_span, token_position):
    for level in range(seg_span.bit_length() - 1):
        partner = swapped(keyval, "seq", level)
        keyval = merge_branch_pair(keyval, partner, level, token_position)
    return keyval


def spread_global(keyval_two):
    keyval_two = lax.all_gather(keyval_two, "seq", axis=1, tiled=True)
    return keyval_two


def combine(partial_value, residual_full, need_full):
    row_count = residual_full.shape[0] // lax.axis_size("mp")
    row_start = lax.axis_index("mp") * row_count
    share = lax.psum_scatter(partial_value, "mp", scatter_dimension=0, tiled=True)
    own_rows = lax.dynamic_slice_in_dim(residual_full, row_start, row_count, 0)
    own_rows = (own_rows.astype(jnp.float32) + share).astype(jnp.bfloat16)
    full_rows = lax.all_gather(own_rows, "mp", axis=0, tiled=True) if need_full else own_rows
    return (own_rows, full_rows)


def body(
    tokens,
    attn_gain,
    query_first,
    key_first,
    segment_value,
    output_first,
    mlp_gain,
    up_weight,
    down_weight,
    second_gain,
    query_second,
    key_second,
    value_second,
    output_second,
    segment_offset,
    global_offset,
):
    seq_count = lax.axis_size("seq")
    token_position = lax.axis_index("seq")
    seg_span = min(SEG_MAX, seq_count)
    head_count = segment_offset.shape[0]
    full_rows = lax.all_gather(tokens, "mp", axis=0, tiled=True)
    token_count = full_rows.shape[0]
    hidden = norm_rows(full_rows.astype(jnp.float32), attn_gain)
    query = jnp.dot(hidden, query_first, preferred_element_type=jnp.float32).astype(jnp.bfloat16)
    seg_stride = token_count // (KEYS // seg_span)
    keyval = pick_keys(hidden, segment_offset, seg_stride, key_first, segment_value)
    keyval = spread_segment(keyval, seg_span, token_position)
    mixed = attend_local(query, keyval, head_count)
    partial_value = jnp.dot(mixed, output_first, preferred_element_type=jnp.float32)
    own_rows, first_rows = combine(partial_value, full_rows, True)
    normed = norm_rows(first_rows.astype(jnp.float32), mlp_gain)
    inner = jax.nn.gelu(
        jnp.dot(normed, up_weight, preferred_element_type=jnp.float32), approximate=True
    ).astype(jnp.bfloat16)
    partial_value = jnp.dot(inner, down_weight, preferred_element_type=jnp.float32)
    own_rows, second_rows = combine(partial_value, first_rows, True)
    hidden_two = norm_rows(second_rows.astype(jnp.float32), second_gain)
    query_two = jnp.dot(hidden_two, query_second, preferred_element_type=jnp.float32).astype(
        jnp.bfloat16
    )
    glob_stride = token_count // (KEYS // seq_count)
    keyval_two = pick_keys(hidden_two, global_offset, glob_stride, key_second, value_second)
    keyval_two = spread_global(keyval_two)
    mixed_two = attend_local(query_two, keyval_two, head_count)
    partial_value = jnp.dot(mixed_two, output_second, preferred_element_type=jnp.float32)
    own_rows, unused_rows = combine(partial_value, second_rows, False)
    return own_rows


MESH = pl.DeviceIdType.MESH
F32 = jnp.float32
BF16 = jnp.bfloat16
WINDOW = 256
LANES = 128
GROUP = 2


def iota(shape, axis):
    return lax.broadcasted_iota(jnp.int32, shape, axis)


def dot32(a, b):
    return jnp.dot(a, b, preferred_element_type=F32)


def dot_last(a, b):
    return lax.dot_general(a, b, (((1,), (1,)), ((), ())), preferred_element_type=F32)


def dot_first(a, b):
    return lax.dot_general(a, b, (((0,), (0,)), ((), ())), preferred_element_type=F32)


def gelu(x):
    slope = math.sqrt(2.0 / math.pi)
    bend = jnp.tanh(x * (x * x * (0.044715 * slope) + slope))
    half = 0.5 * x
    return half * bend + half


class Gather:
    def __init__(self, n, buf, ssem, rsem):
        me = lax.axis_index("seq")
        self.me, self.n, self.high = me, n, n // 4
        self.buf, self.ssem, self.rsem = buf, ssem, rsem
        self.b0, self.b1, self.hi = me % 2, (me // 2) % 2, me // 4
        self.peer1 = self.hi * 4 + (1 - self.b1) * 2 + self.b0
        self.peer0 = self.hi * 4 + self.b1 * 2 + (1 - self.b0)

    def slot(self, d, b1, b0):
        return ((self.hi + self.high - d) % self.high) * 4 + b1 * 2 + b0

    def copy(self, slot, peer, k):
        return pltpu.make_async_remote_copy(
            src_ref=self.buf.at[slot],
            dst_ref=self.buf.at[slot],
            send_sem=self.ssem.at[k],
            recv_sem=self.rsem.at[slot],
            device_id={"seq": peer},
            device_id_type=MESH,
        )

    def far(self, d):
        return ((self.hi + d) % self.high) * 4 + self.b1 * 2 + self.b0

    def peers(self):
        out = [((self.hi + d) % self.high) * 4 + self.b1 * 2 + self.b0 for d in range(1, self.high)]
        return out + [self.peer1, self.peer0]

    def start(self):
        h = self.high
        for d in range(1, h):
            peer = ((self.hi + d) % h) * 4 + self.b1 * 2 + self.b0
            self.copy(self.me, peer, d - 1).start()
        self.copy(self.me, self.peer1, h - 1).start()
        self.copy(self.me, self.peer0, 2 * h - 1).start()

    def second(self, d):
        h = self.high
        slot = self.slot(d, self.b1, self.b0)
        self.copy(slot, self.peer1, h - 1 + d).wait_recv()
        self.copy(slot, self.peer1, h - 1 + d).start()
        self.copy(slot, self.peer0, 2 * h - 1 + d).start()

    def start_across(self):
        self.copy(self.me, self.peer1, 0).start()
        self.copy(self.me, self.peer0, 1).start()
        for d in range(1, self.high):
            self.copy(self.me, self.far(d), 1 + d).start()

    def turn(self):
        slot = self.peer1
        self.copy(slot, self.peer0, 2 * self.high).wait_recv()
        for d in range(1, self.high):
            self.copy(slot, self.far(d), self.high + d).start()
        self.copy(slot, self.peer0, 2 * self.high).start()

    def relay(self, d, b1, k):
        slot = self.slot(d, b1, self.b0)
        self.copy(slot, self.peer0, k).wait_recv()
        self.copy(slot, self.peer0, k).start()

    def third(self, d):
        slot = self.slot(d, 1 - self.b1, self.b0)
        self.copy(slot, self.peer0, 3 * self.high - 1 + d).wait_recv()
        self.copy(slot, self.peer0, 3 * self.high - 1 + d).start()

    def finish(self):
        h = self.high
        for b1 in (self.b1, 1 - self.b1):
            for d in range(h):
                slot = self.slot(d, b1, 1 - self.b0)
                self.copy(slot, self.peer0, 0).wait_recv()
        for k in range(4 * h - 1):
            self.copy(self.me, self.peer0, k).wait_send()


def head_column(offset_ref, heads, picked):
    rows = iota((heads * picked, 1), 0) // picked
    column = jnp.zeros((heads * picked, 1), jnp.int32)
    for h in range(heads):
        column = jnp.where(rows == h, offset_ref[h], column)
    return column


def kernel(
    n, heads, picked, stride,
    seg_hbm, glob_hbm, x_hbm, gain1_hbm, gain_mlp_hbm, gain2_hbm,
    wq1_hbm, wk1_hbm, wv1_hbm, wo1_hbm, up_hbm, down_hbm, wq2_hbm, wk2_hbm, wv2_hbm, wo2_hbm,
    out_hbm,
    seg_ref, glob_ref, x_ref, gain1_ref, gain_mlp_ref, gain2_ref,
    wq1, wk1, wv1, wo1, up, down, wq2, wk2, wv2, wo2,
    xp, q, q_two, normed, key1, value1, kv2, km, vt, perm, perm_back, mix, mix_odd, sem,
    ssemk, rsemk, ssemv, rsemv, ssem2, rsem2,
):
    tokens, width = x_ref.shape
    size = width // heads
    half = LANES // 2
    chunk = heads * picked
    chunks = tokens // chunk
    keys = n * picked
    group = WINDOW // stride
    scale = size ** -0.5 * math.log2(math.e)

    pairs = [(wk1_hbm, wk1), (wv1_hbm, wv1), (wq1_hbm, wq1), (wo1_hbm, wo1), (up_hbm, up),
             (down_hbm, down), (wk2_hbm, wk2), (wv2_hbm, wv2), (wq2_hbm, wq2), (wo2_hbm, wo2),
             (seg_hbm, seg_ref), (x_hbm, x_ref), (gain1_hbm, gain1_ref), (glob_hbm, glob_ref),
             (gain_mlp_hbm, gain_mlp_ref), (gain2_hbm, gain2_ref)]
    loads = [pltpu.make_async_copy(a, b, sem.at[i]) for i, (a, b) in enumerate(pairs)]
    early = (10, 11, 12, 13, 14, 15, 0, 1)
    for i in early:
        loads[i].start()

    key_gather = Gather(n, key1, ssemk, rsemk)
    value_gather = Gather(n, value1, ssemv, rsemv)
    second_gather = Gather(n, kv2, ssem2, rsem2)
    barrier = pltpu.get_barrier_semaphore()
    peers = key_gather.peers()
    for peer in peers:
        pl.semaphore_signal(barrier, inc=1, device_id={"seq": peer}, device_id_type=MESH)

    def own_heads(hidden, weight):
        blocks = []
        for start in range(0, width, WINDOW):
            low, top = start // size, -(-(start + WINDOW) // size)
            full = dot32(hidden[low * picked:top * picked], weight[:, start:start + WINDOW])
            column = iota((picked, WINDOW), 1) + start
            total = jnp.zeros((picked, WINDOW), F32)
            for h in range(low, top):
                mine = (column >= h * size) & (column < h * size + size)
                at = (h - low) * picked
                total = jnp.where(mine, full[at:at + picked], total)
            blocks.append(total)
        return jnp.concatenate(blocks, axis=1).astype(BF16)

    rows = iota((chunk, 1), 0)
    pick = rows % picked
    loads[10].wait()
    target = pick * stride + head_column(seg_ref, heads, picked)
    onehot = (iota((chunk, tokens), 1) == target).astype(F32).astype(BF16)
    loads[11].wait()
    loads[12].wait()
    for i in range(2, 10):
        loads[i].start()
    hidden = norm_rows(dot32(onehot, x_ref[...]), gain1_ref[...][None, :])
    me = key_gather.me
    loads[0].wait()
    key1[me] = own_heads(hidden, wk1)
    pl.semaphore_wait(barrier, len(peers))
    key_gather.start()
    loads[1].wait()
    value1[me] = own_heads(hidden, wv1)
    value_gather.start_across()

    for i in (13, 14, 15):
        loads[i].wait()
    glob_col = head_column(glob_ref, heads, picked)
    lane = iota((16, WINDOW), 1)
    inside = lane % stride
    chosen = jnp.zeros((16, WINDOW), F32)
    for h in range(heads):
        chosen = jnp.where(inside == glob_ref[h], 1.0, chosen)
    a, b = iota((WINDOW, WINDOW), 0), iota((WINDOW, WINDOW), 1)
    same = a // stride == b // stride
    before = jnp.where(same & (a < b), 1.0, 0.0).astype(BF16)
    count = dot32(chosen.astype(BF16), before)
    total = dot32(chosen.astype(BF16), jnp.where(same, 1.0, 0.0).astype(BF16))
    rank = jnp.where(chosen > 0.5, count, total + inside.astype(F32) - count)
    rank_row = rank[0:1, :]
    table = jnp.where(same & (rank_row == (a % stride).astype(F32)), 1.0, 0.0)
    perm[...] = table.astype(BF16)
    perm_back[...] = table.T.astype(BF16)
    at_head = (iota((chunk, WINDOW), 1) == glob_col)
    head_rank = jnp.sum(jnp.where(at_head, rank_row, 0.0), axis=1, keepdims=True)
    spot = (pick * heads).astype(F32) + head_rank
    onehot_two = (iota((chunk, chunk), 1).astype(F32) == spot).astype(F32).astype(BF16)

    for g in range(tokens // WINDOW):
        moved = dot32(perm[...], x_ref[g * WINDOW:(g + 1) * WINDOW, :]).astype(BF16)
        for j in range(group):
            for c in range(chunks):
                at = c * chunk + (g * group + j) * heads
                xp[at:at + heads, :] = moved[j * stride + c * heads:j * stride + (c + 1) * heads]

    def window_of(h):
        return min(h * size // LANES * LANES, width - WINDOW)

    for h in range(heads):
        km[h] = jnp.zeros((WINDOW, keys), BF16)
        vt[h * half + size:(h + 1) * half, :] = jnp.ones((half - size, keys), BF16)

    loads[2].wait()
    loads[3].wait()
    high = key_gather.high

    def query_chunk(c, carry):
        at = pl.ds(pl.multiple_of(c * chunk, chunk), chunk)
        hidden = norm_rows(xp[at, :].astype(F32), gain1_ref[...][None, :])
        q[at, :] = dot32(hidden, wq1[...]).astype(BF16)
        @pl.when(c == 1)
        def _():
            value_gather.turn()

        for d in range(1, high):
            @pl.when(c == d)
            def _(d=d):
                key_gather.second(d)

        return carry

    lax.fori_loop(0, chunks, query_chunk, 0)
    key_gather.third(0)
    for d in range(1, high):
        value_gather.relay(d, value_gather.b1, 2 * high + d)
        key_gather.third(d)
    for d in range(1, high):
        value_gather.relay(d, 1 - value_gather.b1, 3 * high - 1 + d)
    key_gather.finish()
    value_gather.finish()

    def set_keys(key, value):
        for _ in place_keys(key, value):
            pass

    def place_keys(key, value):
        key = key.reshape(keys, width).astype(F32).T.astype(BF16)
        value = value.reshape(keys, width).astype(F32).T.astype(BF16)
        for h in range(heads):
            begin = h * size - window_of(h)
            at = h * size
            km[h, begin:begin + size, :] = key[at:at + size, :]
            vt[h * half:h * half + size, :] = value[at:at + size, :]
            if h % GROUP == 1:
                yield h

    def attend(at, q, mix):
        def score(h):
            start = window_of(h)
            return dot32(q[at, start:start + WINDOW], km[h])

        def soften(scores):
            top = jnp.max(scores, axis=-1, keepdims=True)
            return jnp.exp2((scores - top) * scale).astype(BF16)

        def blend(h, weights):
            both = dot_last(vt[h * half:(h + 1) * half, :], weights)
            mixed = both[:size] * (1.0 / both[size:size + 1])
            mix[h * size:(h + 1) * size, :] = mixed.astype(BF16)

        steps = heads // GROUP
        scores, weights = {}, {}
        for i in range(steps + 2):
            if i < steps:
                for h in range(i * GROUP, (i + 1) * GROUP):
                    scores[h] = score(h)
            if 1 <= i <= steps:
                for h in range((i - 1) * GROUP, i * GROUP):
                    weights[h] = soften(scores.pop(h))
            if i >= 2:
                for h in range((i - 2) * GROUP, (i - 1) * GROUP):
                    blend(h, weights.pop(h))
            yield i

    def rows_of(c):
        return pl.ds(pl.multiple_of(c * chunk, chunk), chunk)

    set_keys(key1[...], value1[...])
    loads[4].wait()
    loads[5].wait()
    loads[6].wait()
    loads[7].wait()
    loads[8].wait()

    def query_two(c):
        at = rows_of(c)
        hidden_two = norm_rows(xp[at, :].astype(F32), gain2_ref[...][None, :])
        for start in range(0, width, WINDOW):
            column = slice(start, start + WINDOW)
            q_two[at, column] = dot32(hidden_two, wq2[:, column]).astype(BF16)
            yield start

    def enter(c):
        at = rows_of(c)
        parts = []
        for start in range(0, width, WINDOW):
            column = slice(start, start + WINDOW)
            parts.append(xp[at, column].astype(F32) + dot_first(mix[...], wo1[:, column]))
            yield start
        first = jnp.concatenate(parts, axis=1).astype(BF16)
        xp[at, :] = first
        normed[...] = norm_rows(first.astype(F32), gain_mlp_ref[...][None, :])

    def first_chunk(c, more, late):
        at = rows_of(c)
        total = xp[at, :].astype(F32)
        blocks = up.shape[1] // WINDOW
        units = {}
        ahead = attend(rows_of(c + 1), q, mix) if more else iter(())
        behind = query_two(late)
        for j in range(blocks + 1):
            if not more and j == blocks // 4:
                second_gather.finish()
                ahead = place_keys(kv2[:, 0:picked, :], kv2[:, picked:2 * picked, :])
            next(ahead, None)
            if j % 3 == 1:
                next(behind, None)
            if j < blocks:
                part = dot32(normed[...], up[:, j * WINDOW:(j + 1) * WINDOW])
                units[j] = gelu(part).astype(BF16)
            if j >= 1:
                total = total + dot32(units.pop(j - 1), down[(j - 1) * WINDOW:j * WINDOW, :])
        for rest in (behind, ahead):
            for _ in rest:
                pass
        second = total.astype(BF16)
        xp[at, :] = second
        if more:
            for _ in enter(c + 1):
                pass
        return second

    for _ in attend(rows_of(0), q, mix):
        pass
    for _ in enter(0):
        pass

    def first_step(c, carry):
        second = first_chunk(c, True, (c + chunks - 1) % chunks)

        @pl.when(c == 0)
        def _():
            rows = dot32(onehot_two, second)
            picked_rows = norm_rows(rows, gain2_ref[...][None, :])
            kv2[me, 0:picked, :] = own_heads(picked_rows, wk2)
            kv2[me, picked:2 * picked, :] = own_heads(picked_rows, wv2)
            second_gather.start()

        @pl.when(c == 1)
        def _():
            for d in range(1, high):
                second_gather.second(d)

        @pl.when(c == 2)
        def _():
            for d in range(high):
                second_gather.third(d)

        return carry

    lax.fori_loop(0, chunks - 1, first_step, 0)
    first_chunk(chunks - 1, False, chunks - 2)
    loads[9].wait()

    def project(c):
        at = rows_of(c)
        for start in range(0, width, WINDOW):
            part = dot_first(mixes[c % 2][...], wo2[:, start:start + WINDOW])
            column = slice(start, start + WINDOW)
            xp[at, column] = (xp[at, column].astype(F32) + part).astype(BF16)
            yield start

    mixes = (mix, mix_odd)
    behind = query_two(chunks - 1)
    for c in range(chunks):
        for i in attend(rows_of(c), q_two, mixes[c % 2]):
            if i >= 1:
                next(behind, None)
        for _ in behind:
            pass
        behind = project(c)
    for _ in behind:
        pass
    stores = []
    for g in range(tokens // WINDOW):
        blocks = []
        for j in range(group):
            for c in range(chunks):
                at = c * chunk + (g * group + j) * heads
                blocks.append(xp[at:at + heads, :])
        moved = dot32(perm_back[...], jnp.concatenate(blocks, axis=0))
        at = slice(g * WINDOW, (g + 1) * WINDOW)
        x_ref[at, :] = moved.astype(BF16)
        stores.append(pltpu.make_async_copy(x_ref.at[at], out_hbm.at[at], sem.at[g]))
        stores[-1].start()
    for store in stores:
        store.wait()


def whole_body(
    tokens, attn_gain, query_first, key_first, segment_value, output_first, mlp_gain, up_weight,
    down_weight, second_gain, query_second, key_second, value_second, output_second,
    segment_offset, global_offset,
):
    n = lax.axis_size("seq")
    heads = segment_offset.shape[0]
    picked = KEYS // n
    count, width = tokens.shape
    stride = count // picked
    units = up_weight.shape[1]
    chunk = heads * picked
    outside = pl.BlockSpec(memory_space=pltpu.HBM)
    square = pltpu.VMEM((width, width), BF16)
    gain = pltpu.VMEM((width,), F32)
    own = pltpu.VMEM((n, picked, width), BF16)
    links = pltpu.SemaphoreType.DMA((n,))
    return pl.pallas_call(
        functools.partial(kernel, n, heads, picked, stride),
        out_shape=jax.ShapeDtypeStruct(tokens.shape, tokens.dtype),
        in_specs=[outside] * 16,
        out_specs=outside,
        scratch_shapes=[
            pltpu.SMEM((heads,), jnp.int32), pltpu.SMEM((heads,), jnp.int32),
            pltpu.VMEM((count, width), BF16),
            gain, gain, gain,
            square, square, square, square,
            pltpu.VMEM((width, units), BF16), pltpu.VMEM((units, width), BF16),
            square, square, square, square,
            pltpu.VMEM((count, width), BF16),
            pltpu.VMEM((count, width), BF16),
            pltpu.VMEM((count, width), BF16),
            pltpu.VMEM((chunk, width), BF16),
            own, own,
            pltpu.VMEM((n, 2 * picked, width), BF16),
            pltpu.VMEM((heads, WINDOW, KEYS), BF16),
            pltpu.VMEM((heads * LANES // 2, KEYS), BF16),
            pltpu.VMEM((WINDOW, WINDOW), BF16),
            pltpu.VMEM((WINDOW, WINDOW), BF16),
            pltpu.VMEM((width, chunk), BF16),
            pltpu.VMEM((width, chunk), BF16),
            pltpu.SemaphoreType.DMA((16,)),
            links, links, links, links, links, links,
        ],
        compiler_params=pltpu.CompilerParams(
            collective_id=0, has_side_effects=True, vmem_limit_bytes=60 << 20
        ),
        name="encoder",
    )(
        segment_offset, global_offset, tokens, attn_gain, mlp_gain, second_gain,
        query_first, key_first, segment_value, output_first, up_weight, down_weight,
        query_second, key_second, value_second, output_second,
    )


def fits(mesh):
    n = mesh.shape["seq"]
    return mesh.shape["mp"] == 1 and n == SEG_MAX


def choose(mesh):
    return whole_body if fits(mesh) else body


def solution(mesh):
    placed = (
        P(("slides", "seq", "mp"), None),
        P(),
        P(None, "mp"),
        P(None, "mp"),
        P(None, "mp"),
        P("mp", None),
        P(),
        P(None, "mp"),
        P("mp", None),
        P(),
        P(None, "mp"),
        P(None, "mp"),
        P(None, "mp"),
        P("mp", None),
        P("mp"),
        P("mp"),
    )
    return jax.shard_map(
        choose(mesh),
        mesh=mesh,
        in_specs=placed,
        out_specs=P(("slides", "seq", "mp"), None),
        check_vma=False,
    )
```

```python
import functools
import math

import jax
import jax.numpy as jnp
from jax import lax
from jax.experimental import pallas as pl
from jax.experimental.pallas import tpu as pltpu
from jax.sharding import PartitionSpec as P

KEYS = 256
SEG_MAX = 16


def swapped(x, axis, apart):
    return lax.ppermute(x, axis, [(i, i ^ 1 << apart) for i in range(lax.axis_size(axis))])


def norm_rows(values, gain):
    center = values - jnp.mean(values, axis=-1, keepdims=True)
    spread = jnp.mean(center * center, axis=-1, keepdims=True)
    return (center * lax.rsqrt(spread + 1e-05) * gain).astype(jnp.bfloat16)


def pick_keys(hidden, offsets, stride, key_weight, value_weight):
    token_count, width = hidden.shape
    head_count = offsets.shape[0]
    head_size = key_weight.shape[1] // head_count
    grouped_rows = hidden.reshape(token_count // stride, stride, width)
    dilation_selector = (
        lax.broadcasted_iota(jnp.int32, (stride, head_count), 0) == offsets[None, :]
    ).astype(jnp.bfloat16)
    chosen = jnp.einsum(
        "nof,oj->njf", grouped_rows, dilation_selector, preferred_element_type=jnp.float32
    ).astype(jnp.bfloat16)
    key_heads = jnp.einsum(
        "xkr,rkf->xkf",
        chosen,
        key_weight.reshape(width, head_count, head_size),
        preferred_element_type=jnp.float32,
    ).astype(jnp.bfloat16)
    value_heads = jnp.einsum(
        "xkr,rkf->xkf",
        chosen,
        value_weight.reshape(width, head_count, head_size),
        preferred_element_type=jnp.float32,
    ).astype(jnp.bfloat16)
    picked = token_count // stride
    return jnp.stack(
        [
            key_heads.reshape(picked, head_count * head_size),
            value_heads.reshape(picked, head_count * head_size),
        ]
    )


def attend_local(query, keyval, head_count):
    token_count, width = query.shape
    head_size = width // head_count
    query_heads = query.reshape(token_count, head_count, head_size)
    key_heads = keyval[0].reshape(-1, head_count, head_size)
    value_heads = keyval[1].reshape(-1, head_count, head_size)
    scores = jnp.einsum(
        "thd,khd->htk", query_heads, key_heads, preferred_element_type=jnp.float32
    ) * head_size ** (-0.5)
    highest = jnp.max(scores, axis=-1, keepdims=True)
    weights = jnp.exp(scores - highest)
    weights = (weights / jnp.sum(weights, axis=-1, keepdims=True)).astype(jnp.bfloat16)
    mixed = jnp.einsum(
        "htk,khd->thd", weights, value_heads, preferred_element_type=jnp.float32
    ).astype(jnp.bfloat16)
    return mixed.reshape(token_count, width)


def merge_branch_pair(mine, other, level, token_position):
    lower = token_position >> level & 1 == 0
    return jnp.where(
        lower, jnp.concatenate((mine, other), axis=1), jnp.concatenate((other, mine), axis=1)
    )


def spread_segment(keyval, seg_span, token_position):
    for level in range(seg_span.bit_length() - 1):
        partner = swapped(keyval, "seq", level)
        keyval = merge_branch_pair(keyval, partner, level, token_position)
    return keyval


def spread_global(keyval_two):
    keyval_two = lax.all_gather(keyval_two, "seq", axis=1, tiled=True)
    return keyval_two


def combine(partial_value, residual_full, need_full):
    row_count = residual_full.shape[0] // lax.axis_size("mp")
    row_start = lax.axis_index("mp") * row_count
    share = lax.psum_scatter(partial_value, "mp", scatter_dimension=0, tiled=True)
    own_rows = lax.dynamic_slice_in_dim(residual_full, row_start, row_count, 0)
    own_rows = (own_rows.astype(jnp.float32) + share).astype(jnp.bfloat16)
    full_rows = lax.all_gather(own_rows, "mp", axis=0, tiled=True) if need_full else own_rows
    return (own_rows, full_rows)


def body(
    tokens,
    attn_gain,
    query_first,
    key_first,
    segment_value,
    output_first,
    mlp_gain,
    up_weight,
    down_weight,
    second_gain,
    query_second,
    key_second,
    value_second,
    output_second,
    segment_offset,
    global_offset,
):
    seq_count = lax.axis_size("seq")
    token_position = lax.axis_index("seq")
    seg_span = min(SEG_MAX, seq_count)
    head_count = segment_offset.shape[0]
    full_rows = lax.all_gather(tokens, "mp", axis=0, tiled=True)
    token_count = full_rows.shape[0]
    hidden = norm_rows(full_rows.astype(jnp.float32), attn_gain)
    query = jnp.dot(hidden, query_first, preferred_element_type=jnp.float32).astype(jnp.bfloat16)
    seg_stride = token_count // (KEYS // seg_span)
    keyval = pick_keys(hidden, segment_offset, seg_stride, key_first, segment_value)
    keyval = spread_segment(keyval, seg_span, token_position)
    mixed = attend_local(query, keyval, head_count)
    partial_value = jnp.dot(mixed, output_first, preferred_element_type=jnp.float32)
    own_rows, first_rows = combine(partial_value, full_rows, True)
    normed = norm_rows(first_rows.astype(jnp.float32), mlp_gain)
    inner = jax.nn.gelu(
        jnp.dot(normed, up_weight, preferred_element_type=jnp.float32), approximate=True
    ).astype(jnp.bfloat16)
    partial_value = jnp.dot(inner, down_weight, preferred_element_type=jnp.float32)
    own_rows, second_rows = combine(partial_value, first_rows, True)
    hidden_two = norm_rows(second_rows.astype(jnp.float32), second_gain)
    query_two = jnp.dot(hidden_two, query_second, preferred_element_type=jnp.float32).astype(
        jnp.bfloat16
    )
    glob_stride = token_count // (KEYS // seq_count)
    keyval_two = pick_keys(hidden_two, global_offset, glob_stride, key_second, value_second)
    keyval_two = spread_global(keyval_two)
    mixed_two = attend_local(query_two, keyval_two, head_count)
    partial_value = jnp.dot(mixed_two, output_second, preferred_element_type=jnp.float32)
    own_rows, unused_rows = combine(partial_value, second_rows, False)
    return own_rows


MESH = pl.DeviceIdType.MESH
F32 = jnp.float32
BF16 = jnp.bfloat16
WINDOW = 256
LANES = 128
GROUP = 2


def iota(shape, axis):
    return lax.broadcasted_iota(jnp.int32, shape, axis)


def dot32(a, b):
    return jnp.dot(a, b, preferred_element_type=F32)


def dot_last(a, b):
    return lax.dot_general(a, b, (((1,), (1,)), ((), ())), preferred_element_type=F32)


def dot_first(a, b):
    return lax.dot_general(a, b, (((0,), (0,)), ((), ())), preferred_element_type=F32)


def gelu(x):
    slope = math.sqrt(2.0 / math.pi)
    bend = jnp.tanh(x * (x * x * (0.044715 * slope) + slope))
    half = 0.5 * x
    return half * bend + half


class Gather:
    def __init__(self, n, buf, ssem, rsem):
        me = lax.axis_index("seq")
        self.me, self.n, self.high = me, n, n // 4
        self.buf, self.ssem, self.rsem = buf, ssem, rsem
        self.b0, self.b1, self.hi = me % 2, (me // 2) % 2, me // 4
        self.peer1 = self.hi * 4 + (1 - self.b1) * 2 + self.b0
        self.peer0 = self.hi * 4 + self.b1 * 2 + (1 - self.b0)

    def slot(self, d, b1, b0):
        return ((self.hi + self.high - d) % self.high) * 4 + b1 * 2 + b0

    def copy(self, slot, peer, k):
        return pltpu.make_async_remote_copy(
            src_ref=self.buf.at[slot],
            dst_ref=self.buf.at[slot],
            send_sem=self.ssem.at[k],
            recv_sem=self.rsem.at[slot],
            device_id={"seq": peer},
            device_id_type=MESH,
        )

    def far(self, d):
        return ((self.hi + d) % self.high) * 4 + self.b1 * 2 + self.b0

    def peers(self):
        out = [((self.hi + d) % self.high) * 4 + self.b1 * 2 + self.b0 for d in range(1, self.high)]
        return out + [self.peer1, self.peer0]

    def start(self):
        h = self.high
        for d in range(1, h):
            peer = ((self.hi + d) % h) * 4 + self.b1 * 2 + self.b0
            self.copy(self.me, peer, d - 1).start()
        self.copy(self.me, self.peer1, h - 1).start()
        self.copy(self.me, self.peer0, 2 * h - 1).start()

    def second(self, d):
        h = self.high
        slot = self.slot(d, self.b1, self.b0)
        self.copy(slot, self.peer1, h - 1 + d).wait_recv()
        self.copy(slot, self.peer1, h - 1 + d).start()
        self.copy(slot, self.peer0, 2 * h - 1 + d).start()

    def start_across(self):
        self.copy(self.me, self.peer1, 0).start()
        self.copy(self.me, self.peer0, 1).start()
        for d in range(1, self.high):
            self.copy(self.me, self.far(d), 1 + d).start()

    def turn(self):
        slot = self.peer1
        self.copy(slot, self.peer0, 2 * self.high).wait_recv()
        for d in range(1, self.high):
            self.copy(slot, self.far(d), self.high + d).start()
        self.copy(slot, self.peer0, 2 * self.high).start()

    def relay(self, d, b1, k):
        slot = self.slot(d, b1, self.b0)
        self.copy(slot, self.peer0, k).wait_recv()
        self.copy(slot, self.peer0, k).start()

    def third(self, d):
        slot = self.slot(d, 1 - self.b1, self.b0)
        self.copy(slot, self.peer0, 3 * self.high - 1 + d).wait_recv()
        self.copy(slot, self.peer0, 3 * self.high - 1 + d).start()

    def finish(self):
        h = self.high
        for b1 in (self.b1, 1 - self.b1):
            for d in range(h):
                slot = self.slot(d, b1, 1 - self.b0)
                self.copy(slot, self.peer0, 0).wait_recv()
        for k in range(4 * h - 1):
            self.copy(self.me, self.peer0, k).wait_send()


def head_column(offset_ref, heads, picked):
    rows = iota((heads * picked, 1), 0) // picked
    column = jnp.zeros((heads * picked, 1), jnp.int32)
    for h in range(heads):
        column = jnp.where(rows == h, offset_ref[h], column)
    return column


def kernel(
    n, heads, picked, stride,
    seg_hbm, glob_hbm, x_hbm, gain1_hbm, gain_mlp_hbm, gain2_hbm,
    wq1_hbm, wk1_hbm, wv1_hbm, wo1_hbm, up_hbm, down_hbm, wq2_hbm, wk2_hbm, wv2_hbm, wo2_hbm,
    out_hbm,
    seg_ref, glob_ref, x_ref, gain1_ref, gain_mlp_ref, gain2_ref,
    wq1, wk1, wv1, wo1, up, down, wq2, wk2, wv2, wo2,
    xp, q, q_two, normed, key1, value1, kv2, km, vt, perm, perm_back, mix, mix_odd, sem,
    ssemk, rsemk, ssemv, rsemv, ssem2, rsem2,
):
    tokens, width = x_ref.shape
    size = width // heads
    half = LANES // 2
    chunk = heads * picked
    chunks = tokens // chunk
    keys = n * picked
    group = WINDOW // stride
    scale = size ** -0.5 * math.log2(math.e)

    pairs = [(wk1_hbm, wk1), (wv1_hbm, wv1), (wq1_hbm, wq1), (wo1_hbm, wo1), (up_hbm, up),
             (down_hbm, down), (wk2_hbm, wk2), (wv2_hbm, wv2), (wq2_hbm, wq2), (wo2_hbm, wo2),
             (seg_hbm, seg_ref), (x_hbm, x_ref), (gain1_hbm, gain1_ref), (glob_hbm, glob_ref),
             (gain_mlp_hbm, gain_mlp_ref), (gain2_hbm, gain2_ref)]
    loads = [pltpu.make_async_copy(a, b, sem.at[i]) for i, (a, b) in enumerate(pairs)]
    early = (10, 11, 12, 13, 14, 15, 0, 1)
    for i in early:
        loads[i].start()

    key_gather = Gather(n, key1, ssemk, rsemk)
    value_gather = Gather(n, value1, ssemv, rsemv)
    second_gather = Gather(n, kv2, ssem2, rsem2)
    barrier = pltpu.get_barrier_semaphore()
    peers = key_gather.peers()
    for peer in peers:
        pl.semaphore_signal(barrier, inc=1, device_id={"seq": peer}, device_id_type=MESH)

    def own_heads(hidden, weight):
        blocks = []
        for start in range(0, width, WINDOW):
            low, top = start // size, -(-(start + WINDOW) // size)
            full = dot32(hidden[low * picked:top * picked], weight[:, start:start + WINDOW])
            column = iota((picked, WINDOW), 1) + start
            total = jnp.zeros((picked, WINDOW), F32)
            for h in range(low, top):
                mine = (column >= h * size) & (column < h * size + size)
                at = (h - low) * picked
                total = jnp.where(mine, full[at:at + picked], total)
            blocks.append(total)
        return jnp.concatenate(blocks, axis=1).astype(BF16)

    rows = iota((chunk, 1), 0)
    pick = rows % picked
    loads[10].wait()
    target = pick * stride + head_column(seg_ref, heads, picked)
    onehot = (iota((chunk, tokens), 1) == target).astype(F32).astype(BF16)
    loads[11].wait()
    loads[12].wait()
    for i in range(2, 10):
        loads[i].start()
    hidden = norm_rows(dot32(onehot, x_ref[...]), gain1_ref[...][None, :])
    me = key_gather.me
    loads[0].wait()
    key1[me] = own_heads(hidden, wk1)
    pl.semaphore_wait(barrier, len(peers))
    key_gather.start()
    loads[1].wait()
    value1[me] = own_heads(hidden, wv1)
    value_gather.start_across()

    for i in (13, 14, 15):
        loads[i].wait()
    glob_col = head_column(glob_ref, heads, picked)
    lane = iota((16, WINDOW), 1)
    inside = lane % stride
    chosen = jnp.zeros((16, WINDOW), F32)
    for h in range(heads):
        chosen = jnp.where(inside == glob_ref[h], 1.0, chosen)
    a, b = iota((WINDOW, WINDOW), 0), iota((WINDOW, WINDOW), 1)
    same = a // stride == b // stride
    before = jnp.where(same & (a < b), 1.0, 0.0).astype(BF16)
    count = dot32(chosen.astype(BF16), before)
    total = dot32(chosen.astype(BF16), jnp.where(same, 1.0, 0.0).astype(BF16))
    rank = jnp.where(chosen > 0.5, count, total + inside.astype(F32) - count)
    rank_row = rank[0:1, :]
    table = jnp.where(same & (rank_row == (a % stride).astype(F32)), 1.0, 0.0)
    perm[...] = table.astype(BF16)
    perm_back[...] = table.T.astype(BF16)
    at_head = (iota((chunk, WINDOW), 1) == glob_col)
    head_rank = jnp.sum(jnp.where(at_head, rank_row, 0.0), axis=1, keepdims=True)
    spot = (pick * heads).astype(F32) + head_rank
    onehot_two = (iota((chunk, chunk), 1).astype(F32) == spot).astype(F32).astype(BF16)

    for g in range(tokens // WINDOW):
        moved = dot32(perm[...], x_ref[g * WINDOW:(g + 1) * WINDOW, :]).astype(BF16)
        for j in range(group):
            for c in range(chunks):
                at = c * chunk + (g * group + j) * heads
                xp[at:at + heads, :] = moved[j * stride + c * heads:j * stride + (c + 1) * heads]

    def window_of(h):
        return min(h * size // LANES * LANES, width - WINDOW)

    for h in range(heads):
        km[h] = jnp.zeros((WINDOW, keys), BF16)
        vt[h * half + size:(h + 1) * half, :] = jnp.ones((half - size, keys), BF16)

    loads[2].wait()
    loads[3].wait()
    high = key_gather.high

    def query_chunk(c, carry):
        at = pl.ds(pl.multiple_of(c * chunk, chunk), chunk)
        hidden = norm_rows(xp[at, :].astype(F32), gain1_ref[...][None, :])
        q[at, :] = dot32(hidden, wq1[...]).astype(BF16)
        @pl.when(c == 1)
        def _():
            value_gather.turn()

        for d in range(1, high):
            @pl.when(c == d)
            def _(d=d):
                key_gather.second(d)

        return carry

    lax.fori_loop(0, chunks, query_chunk, 0)
    key_gather.third(0)
    for d in range(1, high):
        value_gather.relay(d, value_gather.b1, 2 * high + d)
        key_gather.third(d)
    for d in range(1, high):
        value_gather.relay(d, 1 - value_gather.b1, 3 * high - 1 + d)
    key_gather.finish()
    value_gather.finish()

    def set_keys(key, value):
        for _ in place_keys(key, value):
            pass

    def place_keys(key, value):
        key = key.reshape(keys, width).astype(F32).T.astype(BF16)
        value = value.reshape(keys, width).astype(F32).T.astype(BF16)
        for h in range(heads):
            begin = h * size - window_of(h)
            at = h * size
            km[h, begin:begin + size, :] = key[at:at + size, :]
            vt[h * half:h * half + size, :] = value[at:at + size, :]
            if h % GROUP == 1:
                yield h

    def attend(at, q, mix):
        def score(h):
            start = window_of(h)
            return dot32(q[at, start:start + WINDOW], km[h])

        def soften(scores):
            top = jnp.max(scores, axis=-1, keepdims=True)
            return jnp.exp2((scores - top) * scale).astype(BF16)

        def blend(h, weights):
            both = dot_last(vt[h * half:(h + 1) * half, :], weights)
            mixed = both[:size] * (1.0 / both[size:size + 1])
            mix[h * size:(h + 1) * size, :] = mixed.astype(BF16)

        steps = heads // GROUP
        scores, weights = {}, {}
        for i in range(steps + 2):
            if i < steps:
                for h in range(i * GROUP, (i + 1) * GROUP):
                    scores[h] = score(h)
            if 1 <= i <= steps:
                for h in range((i - 1) * GROUP, i * GROUP):
                    weights[h] = soften(scores.pop(h))
            if i >= 2:
                for h in range((i - 2) * GROUP, (i - 1) * GROUP):
                    blend(h, weights.pop(h))
            yield i

    def rows_of(c):
        return pl.ds(pl.multiple_of(c * chunk, chunk), chunk)

    set_keys(key1[...], value1[...])
    loads[4].wait()
    loads[5].wait()
    loads[6].wait()
    loads[7].wait()
    loads[8].wait()

    def query_two(c):
        at = rows_of(c)
        hidden_two = norm_rows(xp[at, :].astype(F32), gain2_ref[...][None, :])
        for start in range(0, width, WINDOW):
            column = slice(start, start + WINDOW)
            q_two[at, column] = dot32(hidden_two, wq2[:, column]).astype(BF16)
            yield start

    def enter(c):
        at = rows_of(c)
        parts = []
        for start in range(0, width, WINDOW):
            column = slice(start, start + WINDOW)
            parts.append(xp[at, column].astype(F32) + dot_first(mix[...], wo1[:, column]))
            yield start
        first = jnp.concatenate(parts, axis=1).astype(BF16)
        xp[at, :] = first
        normed[...] = norm_rows(first.astype(F32), gain_mlp_ref[...][None, :])

    def first_chunk(c, more, late):
        at = rows_of(c)
        total = xp[at, :].astype(F32)
        blocks = up.shape[1] // WINDOW
        units = {}
        ahead = attend(rows_of(c + 1), q, mix) if more else iter(())
        behind = query_two(late)
        entering = enter(c + 1) if more else iter(())
        done = heads // GROUP + 2
        for j in range(blocks + 1):
            if not more and j == blocks // 4:
                second_gather.finish()
                ahead = place_keys(kv2[:, 0:picked, :], kv2[:, picked:2 * picked, :])
            next(ahead, None)
            if j % 3 == 1:
                next(behind, None)
            if j >= done:
                next(entering, None)
            if j < blocks:
                part = dot32(normed[...], up[:, j * WINDOW:(j + 1) * WINDOW])
                units[j] = gelu(part).astype(BF16)
            if j >= 1:
                total = total + dot32(units.pop(j - 1), down[(j - 1) * WINDOW:j * WINDOW, :])
        for rest in (behind, ahead):
            for _ in rest:
                pass
        second = total.astype(BF16)
        xp[at, :] = second
        for _ in entering:
            pass
        return second

    for _ in attend(rows_of(0), q, mix):
        pass
    for _ in enter(0):
        pass

    def first_step(c, carry):
        second = first_chunk(c, True, (c + chunks - 1) % chunks)

        @pl.when(c == 0)
        def _():
            rows = dot32(onehot_two, second)
            picked_rows = norm_rows(rows, gain2_ref[...][None, :])
            kv2[me, 0:picked, :] = own_heads(picked_rows, wk2)
            kv2[me, picked:2 * picked, :] = own_heads(picked_rows, wv2)
            second_gather.start()

        @pl.when(c == 1)
        def _():
            for d in range(1, high):
                second_gather.second(d)

        @pl.when(c == 2)
        def _():
            for d in range(high):
                second_gather.third(d)

        return carry

    lax.fori_loop(0, chunks - 1, first_step, 0)
    first_chunk(chunks - 1, False, chunks - 2)
    loads[9].wait()

    def project(c):
        at = rows_of(c)
        for start in range(0, width, WINDOW):
            part = dot_first(mixes[c % 2][...], wo2[:, start:start + WINDOW])
            column = slice(start, start + WINDOW)
            xp[at, column] = (xp[at, column].astype(F32) + part).astype(BF16)
            yield start

    mixes = (mix, mix_odd)
    behind = query_two(chunks - 1)
    for c in range(chunks):
        for i in attend(rows_of(c), q_two, mixes[c % 2]):
            if i >= 1:
                next(behind, None)
        for _ in behind:
            pass
        behind = project(c)
    for _ in behind:
        pass
    stores = []
    for g in range(tokens // WINDOW):
        blocks = []
        for j in range(group):
            for c in range(chunks):
                at = c * chunk + (g * group + j) * heads
                blocks.append(xp[at:at + heads, :])
        moved = dot32(perm_back[...], jnp.concatenate(blocks, axis=0))
        at = slice(g * WINDOW, (g + 1) * WINDOW)
        x_ref[at, :] = moved.astype(BF16)
        stores.append(pltpu.make_async_copy(x_ref.at[at], out_hbm.at[at], sem.at[g]))
        stores[-1].start()
    for store in stores:
        store.wait()


def whole_body(
    tokens, attn_gain, query_first, key_first, segment_value, output_first, mlp_gain, up_weight,
    down_weight, second_gain, query_second, key_second, value_second, output_second,
    segment_offset, global_offset,
):
    n = lax.axis_size("seq")
    heads = segment_offset.shape[0]
    picked = KEYS // n
    count, width = tokens.shape
    stride = count // picked
    units = up_weight.shape[1]
    chunk = heads * picked
    outside = pl.BlockSpec(memory_space=pltpu.HBM)
    square = pltpu.VMEM((width, width), BF16)
    gain = pltpu.VMEM((width,), F32)
    own = pltpu.VMEM((n, picked, width), BF16)
    links = pltpu.SemaphoreType.DMA((n,))
    return pl.pallas_call(
        functools.partial(kernel, n, heads, picked, stride),
        out_shape=jax.ShapeDtypeStruct(tokens.shape, tokens.dtype),
        in_specs=[outside] * 16,
        out_specs=outside,
        scratch_shapes=[
            pltpu.SMEM((heads,), jnp.int32), pltpu.SMEM((heads,), jnp.int32),
            pltpu.VMEM((count, width), BF16),
            gain, gain, gain,
            square, square, square, square,
            pltpu.VMEM((width, units), BF16), pltpu.VMEM((units, width), BF16),
            square, square, square, square,
            pltpu.VMEM((count, width), BF16),
            pltpu.VMEM((count, width), BF16),
            pltpu.VMEM((count, width), BF16),
            pltpu.VMEM((chunk, width), BF16),
            own, own,
            pltpu.VMEM((n, 2 * picked, width), BF16),
            pltpu.VMEM((heads, WINDOW, KEYS), BF16),
            pltpu.VMEM((heads * LANES // 2, KEYS), BF16),
            pltpu.VMEM((WINDOW, WINDOW), BF16),
            pltpu.VMEM((WINDOW, WINDOW), BF16),
            pltpu.VMEM((width, chunk), BF16),
            pltpu.VMEM((width, chunk), BF16),
            pltpu.SemaphoreType.DMA((16,)),
            links, links, links, links, links, links,
        ],
        compiler_params=pltpu.CompilerParams(
            collective_id=0, has_side_effects=True, vmem_limit_bytes=60 << 20
        ),
        name="encoder",
    )(
        segment_offset, global_offset, tokens, attn_gain, mlp_gain, second_gain,
        query_first, key_first, segment_value, output_first, up_weight, down_weight,
        query_second, key_second, value_second, output_second,
    )


def fits(mesh):
    n = mesh.shape["seq"]
    return mesh.shape["mp"] == 1 and n == SEG_MAX


def choose(mesh):
    return whole_body if fits(mesh) else body


def solution(mesh):
    placed = (
        P(("slides", "seq", "mp"), None),
        P(),
        P(None, "mp"),
        P(None, "mp"),
        P(None, "mp"),
        P("mp", None),
        P(),
        P(None, "mp"),
        P("mp", None),
        P(),
        P(None, "mp"),
        P(None, "mp"),
        P(None, "mp"),
        P("mp", None),
        P("mp"),
        P("mp"),
    )
    return jax.shard_map(
        choose(mesh),
        mesh=mesh,
        in_specs=placed,
        out_specs=P(("slides", "seq", "mp"), None),
        check_vma=False,
    )
```
